128 devices in a mesh: outer: 4 (over x_hi, core), inner: 32 (over y, z, x_lo).
Axes of the slice: x: 4 (x_hi: 2, x_lo: 2; x = x_hi * 2 + x_lo), y: 4, z: 4, core: 2. Of those that a mesh axis runs over, the one named last changes fastest.
Arguments:
- projected: bfloat16 [16384, 12288], P(('outer', 'inner')), may hold values from -6 to 6
- short_filter: bfloat16 [3, 12288], replicated, may hold values from -3.5 to 3.5
- long_filter: bfloat16 [16384, 4096], P(('outer', 'inner')), may hold values from 0 to 0.35
- skip: float32 [4096], replicated, may hold values from 0.1 to 1.9
Outputs:
- mixed: bfloat16 [16384, 4096], P(('outer', 'inner'))
The draws below stay inside these ranges and needn't reach their ends.
All inputs are finite; a program needn't handle non-finite values.
Results may differ from the reference program's by a relative error of at most 0.0075.
Values may be sent and summed in bfloat16 or wider, within the bound.
No kernel may reach another device: no remote copies, remote signals or barrier semaphores. Data moves between devices by JAX's collectives and lax.ppermute only.
A program may use at most 128 MiB of HBM per device.

```python
import math
import jax
import jax.numpy as jnp
from jax import lax

C = 4096
SHORT = 3
TOK_DEV = 128
SEQ = 16384
BLOCKS = 256
TRANSFORM = 32768
N_OUTER = 4
N_INNER = 32


def draw_long_filter(key, part):
    keys = jax.random.split(key, 6)
    slow_share = 0.5
    lower_rough = 0.5
    upper_rough = 1.5
    slow_mask = jax.random.uniform(keys[0], (C,)) < slow_share
    slow_log = jax.random.uniform(keys[1], (C,), minval=math.log(0.5 / SEQ), maxval=math.log(2.0 / SEQ))
    fast_log = jax.random.uniform(keys[2], (C,), minval=math.log(1.0 / 400.0), maxval=math.log(1.0 / 30.0))
    decay_rate = jnp.exp(jnp.where(slow_mask, slow_log, fast_log))
    lag_index = jnp.arange(SEQ, dtype=jnp.int32)[:, None]
    positions = lag_index.astype(jnp.float32)
    roughness = jax.random.uniform(keys[3], (SEQ, C), minval=lower_rough, maxval=upper_rough)
    echo_rough = jax.random.uniform(keys[4], (SEQ, C), minval=lower_rough, maxval=upper_rough)
    delay = jax.random.randint(keys[5], (C,), SEQ // 8, SEQ // 2 + 1).astype(jnp.int32)
    main_part = jnp.sqrt(decay_rate)[None, :] * jnp.exp(-decay_rate[None, :] * positions) * roughness
    since_delay = jnp.maximum(lag_index - delay[None, :], 0).astype(jnp.float32)
    echo_live = jnp.logical_and(lag_index >= delay[None, :], jnp.logical_not(slow_mask)[None, :])
    echo_part = 0.5 * jnp.sqrt(decay_rate)[None, :] * jnp.exp(-decay_rate[None, :] * since_delay) * echo_rough
    filter_taps = main_part + jnp.where(echo_live, echo_part, 0.0)
    return filter_taps.astype(jnp.bfloat16)


def block_scale(stream_key, extent, cuts, smallest, largest):
    loudness, own = 1.0, jax.random.fold_in(stream_key, 6)
    for dim, shards_of in cuts:
        draws = jnp.exp(jax.random.uniform(jax.random.fold_in(own, dim), (shards_of,), jnp.float32, smallest / len(cuts), largest / len(cuts)))
        loudness = loudness * jnp.repeat(draws, extent[dim] // shards_of).reshape([-1 if axis == dim else 1 for axis in range(len(extent))])
    return loudness


def gaussian(stream_key, shape, scale, most, cuts=(), held_as=jnp.bfloat16):
    result = scale * jax.random.normal(stream_key, shape, jnp.float32)
    if cuts:
        result = result * block_scale(stream_key, shape, cuts, -0.22, 0.18)
    return jnp.clip(result, -most, most).astype(held_as)


def setup_inputs(seed: int = 0) -> dict:
    splits = jax.random.split(jax.random.key(seed), 5)
    return {
        "projected": gaussian(splits[0], (SEQ, 3 * C), 1.0, 6.0, ((0, 128),)),
        "short_filter": gaussian(splits[1], (SHORT, 3 * C), SHORT ** -0.5, 3.5),
        "long_filter": draw_long_filter(jax.random.fold_in(splits[4], 71), 0),
        "skip": jnp.clip(1.0 + 0.18 * jax.random.normal(splits[3], (C,), jnp.float32), 0.1, 1.9),
    }


TWO_PI = 2.0 * math.pi


def turn_table(rows, cols, length):
    product = (rows * cols) % length
    angle = product.astype(jnp.float32) * (TWO_PI / length)
    return jnp.cos(angle), jnp.sin(angle)


def counting(count):
    return jnp.arange(count, dtype=jnp.int32)


def rounded(table):
    narrow = lax.optimization_barrier(table.astype(jnp.bfloat16))
    return narrow.astype(jnp.float32)


def widened(values):
    return values.astype(jnp.float32)


def reference(projected, short_filter, long_filter, skip):
    segments = N_OUTER * N_INNER
    tap_count = short_filter.shape[0]
    width_block = math.gcd(C, 128)
    block_count = C // width_block
    cos_first, sin_first = turn_table(counting(BLOCKS)[:, None], counting(segments)[None, :], BLOCKS)
    cos_first, sin_first = rounded(cos_first), rounded(sin_first)
    cos_local, sin_local = turn_table(counting(TOK_DEV)[:, None], counting(TOK_DEV)[None, :], TOK_DEV)
    cos_local, sin_local = rounded(cos_local), rounded(sin_local)
    cos_last, sin_last = turn_table(counting(segments)[:, None], counting(BLOCKS)[None, :], BLOCKS)
    cos_last, sin_last = rounded(cos_last), rounded(sin_last)
    turn_cos, turn_sin = turn_table(counting(BLOCKS)[:, None], counting(TOK_DEV)[None, :], TRANSFORM)
    turn_cos = turn_cos[:, :, None]
    turn_sin = turn_sin[:, :, None]

    def featurize(columns, weights):
        padded = jnp.concatenate([jnp.zeros((tap_count - 1, width_block), jnp.bfloat16), columns], 0)
        summed = jnp.zeros((SEQ, width_block), jnp.float32)
        for tap_index in range(tap_count):
            offset = tap_count - 1 - tap_index
            summed = summed + weights[tap_index].astype(jnp.float32) * padded[offset:offset + SEQ].astype(jnp.float32)
        return summed

    def first_section(values):
        stacked = widened(values.reshape(segments, TOK_DEV, width_block))
        real_part = jnp.einsum('kb,bac->kac', cos_first, stacked)
        imag_part = -jnp.einsum('kb,bac->kac', sin_first, stacked)
        out_real = (real_part * turn_cos + imag_part * turn_sin).astype(jnp.bfloat16)
        out_imag = (imag_part * turn_cos - real_part * turn_sin).astype(jnp.bfloat16)
        return out_real, out_imag

    def local_section(real_half, imag_half):
        real_part = widened(real_half)
        imag_part = widened(imag_half)
        spec_real = jnp.einsum('ua,kac->kuc', cos_local, real_part) + jnp.einsum('ua,kac->kuc', sin_local, imag_part)
        spec_imag = jnp.einsum('ua,kac->kuc', cos_local, imag_part) - jnp.einsum('ua,kac->kuc', sin_local, real_part)
        return spec_real, spec_imag

    def one_block(block_index):
        offset = block_index * width_block
        query_cols = lax.dynamic_slice_in_dim(projected, offset, width_block, 1)
        key_cols = lax.dynamic_slice_in_dim(projected, offset + C, width_block, 1)
        value_cols = lax.dynamic_slice_in_dim(projected, offset + 2 * C, width_block, 1)
        query_taps = lax.dynamic_slice_in_dim(short_filter, offset, width_block, 1)
        key_taps = lax.dynamic_slice_in_dim(short_filter, offset + C, width_block, 1)
        value_taps = lax.dynamic_slice_in_dim(short_filter, offset + 2 * C, width_block, 1)
        query_rows = featurize(query_cols, query_taps)
        gated_rows = (featurize(key_cols, key_taps) * featurize(value_cols, value_taps)).astype(jnp.bfloat16)
        filter_cols = lax.dynamic_slice_in_dim(long_filter, offset, width_block, 1)
        signal_real, signal_imag = local_section(*first_section(gated_rows))
        filter_real, filter_imag = local_section(*first_section(filter_cols))
        product_real = widened((signal_real * filter_real - signal_imag * filter_imag).astype(jnp.bfloat16))
        product_imag = widened((signal_real * filter_imag + signal_imag * filter_real).astype(jnp.bfloat16))
        back_real = jnp.einsum('au,kuc->kac', cos_local, product_real) - jnp.einsum('au,kuc->kac', sin_local, product_imag)
        back_imag = jnp.einsum('au,kuc->kac', cos_local, product_imag) + jnp.einsum('au,kuc->kac', sin_local, product_real)
        first_real = widened((back_real * turn_cos - back_imag * turn_sin).astype(jnp.bfloat16))
        first_imag = widened((back_imag * turn_cos + back_real * turn_sin).astype(jnp.bfloat16))
        long_conv = (jnp.einsum('bk,kac->bac', cos_last, first_real) - jnp.einsum('bk,kac->bac', sin_last, first_imag)) * (1.0 / TRANSFORM)
        long_conv = long_conv.astype(jnp.bfloat16).reshape(SEQ, width_block)
        skip_gain = lax.dynamic_slice_in_dim(skip, offset, width_block, 0)
        mixed_cols = query_rows * (long_conv.astype(jnp.float32) + skip_gain[None, :] * gated_rows.astype(jnp.float32))
        return mixed_cols.astype(jnp.bfloat16)

    outputs = lax.map(one_block, counting(block_count))
    return jnp.transpose(outputs, (1, 0, 2)).reshape(SEQ, C)
```

```python
import math

import jax
import jax.numpy as jnp
import numpy as np
from jax import lax
from jax.experimental import pallas as pl
from jax.experimental.pallas import tpu as pltpu
from jax.sharding import PartitionSpec as P

AXES = ("outer", "inner")
F32 = jnp.float32
BF16 = jnp.bfloat16


def turn_table(rows, cols, length):
    product = (np.asarray(rows, np.int64) * np.asarray(cols, np.int64)) % length
    angle = product.astype(np.float32) * np.float32(2.0 * math.pi / length)
    angle = angle.astype(np.float64)
    return np.cos(angle).astype(np.float32), np.sin(angle).astype(np.float32)


def tables(segments, tok):
    half = segments
    blocks = 2 * segments
    transform = blocks * tok
    kb = np.arange(half + 1)
    cos_b, sin_b = turn_table(kb[:, None], np.arange(segments)[None, :], blocks)
    first = np.concatenate([cos_b[:half], cos_b[half:], -sin_b[1:half]], 0)
    weight = np.full((half + 1,), 2.0, np.float32)
    weight[0] = weight[half] = 1.0
    cos_w = cos_b.astype(BF16).astype(np.float32) * weight[:, None]
    sin_w = sin_b.astype(BF16).astype(np.float32) * weight[:, None]
    last = np.concatenate([cos_w[:half], cos_w[half:], -sin_w[1:half]], 0).T
    cos_l, sin_l = turn_table(np.arange(tok)[:, None], np.arange(tok)[None, :], tok)
    forward = np.block([[cos_l, -sin_l], [sin_l, cos_l]])
    backward = np.block([[cos_l, sin_l], [-sin_l, cos_l]])
    turn_cos, turn_sin = turn_table(kb[:, None], np.arange(tok)[None, :], transform)
    return (
        first.astype(BF16),
        forward.astype(BF16),
        backward.astype(BF16),
        last.astype(BF16),
        turn_cos[:half],
        turn_sin[:half],
        turn_cos[half:],
        turn_sin[half:],
    )


def featurized(rows, rim, taps):
    rows = rows.astype(F32)
    rim = rim.astype(F32)
    taps = taps.astype(F32)
    index = lax.broadcasted_iota(jnp.int32, rows.shape, 0)
    back1 = jnp.where(index == 0, rim[1:2], pltpu.roll(rows, 1, 0))
    back2 = pltpu.roll(rows, 2, 0)
    back2 = jnp.where(index == 0, rim[0:1], jnp.where(index == 1, rim[1:2], back2))
    return taps[0:1] * rows + taps[1:2] * back1 + taps[2:3] * back2


def gate_kernel(k_ref, v_ref, rk_ref, rv_ref, wk_ref, wv_ref, f_ref, send_ref, gated_ref):
    gated = featurized(k_ref[...], rk_ref[...], wk_ref[...]) * featurized(
        v_ref[...], rv_ref[...], wv_ref[...]
    )
    gated = gated.astype(BF16)
    gated_ref[...] = gated
    dests, twice, tok = send_ref.shape
    own = twice // 2
    send_ref[:, :own, :] = gated.T.reshape(dests, own, tok)
    send_ref[:, own:, :] = f_ref[...].T.reshape(dests, own, tok)


def gate(projected, rim, short_filter, long_filter, devices):
    tok, width = long_filter.shape
    own = width // devices
    steps = 8
    cols = width // steps
    peers = devices // steps

    def col(third):
        return lambda i: (0, i + third * steps)

    return pl.pallas_call(
        gate_kernel,
        grid=(steps,),
        in_specs=[
            pl.BlockSpec((tok, cols), col(1)),
            pl.BlockSpec((tok, cols), col(2)),
            pl.BlockSpec((rim.shape[0], cols), col(1)),
            pl.BlockSpec((rim.shape[0], cols), col(2)),
            pl.BlockSpec((short_filter.shape[0], cols), col(1)),
            pl.BlockSpec((short_filter.shape[0], cols), col(2)),
            pl.BlockSpec((tok, cols), lambda i: (0, i)),
        ],
        out_specs=[
            pl.BlockSpec((peers, 2 * own, tok), lambda i: (i, 0, 0)),
            pl.BlockSpec((tok, cols), lambda i: (0, i)),
        ],
        out_shape=[
            jax.ShapeDtypeStruct((devices, 2 * own, tok), BF16),
            jax.ShapeDtypeStruct((tok, width), BF16),
        ],
        name="gate",
    )(projected, projected, rim, rim, short_filter, short_filter, long_filter)


def dot(a, b):
    return jnp.dot(a, b, preferred_element_type=F32)


def spectral_kernel(
    z_ref, first_ref, fwd_ref, bwd_ref, last_ref, tc_ref, ts_ref, hc_ref, hs_ref, out_ref,
    rows_ref, spec_ref, half_ref, half_out_ref, conv_ref,
):
    segments, both, tok = z_ref.shape
    own = both // 2
    piece = 16

    def widen(i, carry):
        start = pl.multiple_of(i * piece, piece)
        block = z_ref[pl.ds(start, piece)].astype(F32).reshape(piece * both, tok)
        rows_ref[pl.ds(pl.multiple_of(start * both, piece * both), piece * both), :] = block
        return carry

    lax.fori_loop(0, segments // piece, widen, 0)

    index = lax.broadcasted_iota(jnp.int32, (segments, tok), 0)
    group = 4

    def first_section(i, carry):
        cols = [
            rows_ref[pl.ds(i * group + j, segments, stride=both), :].astype(BF16)
            for j in range(group)
        ]
        out = dot(first_ref[...], jnp.concatenate(cols, 1))
        tc, ts = tc_ref[...], ts_ref[...]
        for j in range(group):
            real = out[:segments, j * tok : (j + 1) * tok]
            imag = out[segments:, j * tok : (j + 1) * tok]
            half_ref[pl.ds(i * group + j, 1), :] = imag[0:1]
            imag = jnp.where(index == 0, 0.0, imag)
            spec_ref[i * group + j, :, :tok] = (real * tc + imag * ts).astype(BF16)
            spec_ref[i * group + j, :, tok:] = (imag * tc - real * ts).astype(BF16)
        return carry

    lax.fori_loop(0, both // group, first_section, 0)

    def product(sig, fil):
        sr, si, fr, fi = sig[:, :tok], sig[:, tok:], fil[:, :tok], fil[:, tok:]
        return jnp.concatenate(
            [(sr * fr - si * fi).astype(BF16), (sr * fi + si * fr).astype(BF16)], 1
        )

    half = half_ref[...]
    hc, hs = hc_ref[...], hs_ref[...]
    half = jnp.concatenate([(half * hc).astype(BF16), (-half * hs).astype(BF16)], 1)
    half = dot(half, fwd_ref[...])
    half = dot(product(half[:own], half[own:]), bwd_ref[...])
    half_out_ref[...] = half[:, :tok] * hc - half[:, tok:] * hs

    scale = 1.0 / (2 * segments * tok)

    def middle(i, carry):
        tc, ts = tc_ref[...], ts_ref[...]
        reals, imags = [], []
        for j in range(2):
            c = i * 2 + j
            sig = dot(spec_ref[c], fwd_ref[...])
            fil = dot(spec_ref[own + c], fwd_ref[...])
            back = dot(product(sig, fil), bwd_ref[...])
            br, bi = back[:, :tok], back[:, tok:]
            imag = jnp.where(index == 0, half_out_ref[pl.ds(c, 1), :], bi * tc + br * ts)
            reals.append((br * tc - bi * ts).astype(BF16))
            imags.append(imag.astype(BF16))
        stacked = jnp.concatenate(
            [jnp.concatenate(reals, 1), jnp.concatenate(imags, 1)], 0
        )
        conv = dot(last_ref[...], stacked) * scale
        for j in range(2):
            conv_ref[pl.ds(i * 2 + j, segments, stride=own), :] = conv[:, j * tok : (j + 1) * tok]
        return carry

    lax.fori_loop(0, own // 2, middle, 0)

    def narrow(i, carry):
        start = pl.multiple_of(i * piece, piece)
        block = conv_ref[pl.ds(pl.multiple_of(start * own, piece * own), piece * own), :]
        out_ref[pl.ds(start, piece)] = block.astype(BF16).reshape(piece, own, tok)
        return carry

    lax.fori_loop(0, segments // piece, narrow, 0)


def spectral(received, consts):
    segments, both, tok = received.shape
    own = both // 2
    return pl.pallas_call(
        spectral_kernel,
        out_shape=jax.ShapeDtypeStruct((segments, own, tok), BF16),
        in_specs=[pl.BlockSpec(memory_space=pltpu.VMEM)] * 9,
        out_specs=pl.BlockSpec(memory_space=pltpu.VMEM),
        scratch_shapes=[
            pltpu.VMEM((segments * both, tok), F32),
            pltpu.VMEM((both, segments, 2 * tok), BF16),
            pltpu.VMEM((both, tok), F32),
            pltpu.VMEM((own, tok), F32),
            pltpu.VMEM((segments * own, tok), F32),
        ],
        name="spectral",
    )(received, *consts)


def mix_kernel(c_ref, q_ref, s_ref, out_ref):
    peers, own, tok = c_ref.shape
    conv = c_ref[...].reshape(peers * own, tok).T.astype(F32)
    out_ref[...] = (q_ref[...] * (conv + s_ref[...])).astype(BF16)


def mix(conv, query, direct):
    devices, own, tok = conv.shape
    width = devices * own
    steps = 8
    cols = width // steps
    wide = pl.BlockSpec((tok, cols), lambda i: (0, i))
    return pl.pallas_call(
        mix_kernel,
        grid=(steps,),
        in_specs=[pl.BlockSpec((devices // steps, own, tok), lambda i: (i, 0, 0)), wide, wide],
        out_specs=wide,
        out_shape=jax.ShapeDtypeStruct((tok, width), BF16),
        name="mix",
    )(conv, query, direct)


def shards(projected, short_filter, long_filter, skip):
    devices = lax.axis_size(AXES)
    tok, width = long_filter.shape
    tap_count = short_filter.shape[0]
    rim_count = tap_count - 1
    consts = tables(devices, tok)
    rim = lax.ppermute(
        projected[tok - rim_count :], AXES, [(i, i + 1) for i in range(devices - 1)]
    )
    send, gated = gate(projected, rim, short_filter, long_filter, devices)
    received = lax.all_to_all(send, AXES, split_axis=0, concat_axis=0, tiled=True)
    extended = jnp.concatenate([rim[:, :width], projected[:, :width]], 0).astype(F32)
    query = jnp.zeros((tok, width), F32)
    for tap in range(tap_count):
        offset = rim_count - tap
        query = query + short_filter[tap, :width].astype(F32) * extended[offset : offset + tok]
    direct = skip[None, :] * gated.astype(F32)
    conv = spectral(received, consts)
    conv = lax.all_to_all(conv, AXES, split_axis=0, concat_axis=0, tiled=True)
    return mix(conv, query, direct)


def solution(mesh):
    in_specs = (P(AXES, None), P(), P(AXES, None), P())
    return jax.shard_map(
        shards, mesh=mesh, in_specs=in_specs, out_specs=P(AXES, None), check_vma=False
    )
```

```python
import functools
import math

import jax
import jax.numpy as jnp
import numpy as np
from jax import lax
from jax.experimental import pallas as pl
from jax.experimental.pallas import tpu as pltpu
from jax.sharding import PartitionSpec as P

AXES = ("outer", "inner")
F32 = jnp.float32
BF16 = jnp.bfloat16
PAD = 1


def turn_table(rows, cols, length):
    product = (np.asarray(rows, np.int64) * np.asarray(cols, np.int64)) % length
    angle = product.astype(np.float32) * np.float32(2.0 * math.pi / length)
    angle = angle.astype(np.float64)
    return np.cos(angle).astype(np.float32), np.sin(angle).astype(np.float32)


def paired(reals, imags):
    both = np.stack([reals.reshape(-1, 8, reals.shape[1]), imags.reshape(-1, 8, imags.shape[1])], 1)
    return both.reshape(-1, reals.shape[1])


def tables(segments, tok):
    half = segments
    blocks = 2 * segments
    transform = blocks * tok
    kb = np.arange(half + 1)
    cos_b, sin_b = turn_table(kb[:, None], np.arange(segments)[None, :], blocks)
    first = paired(cos_b[:half], np.concatenate([cos_b[half:], -sin_b[1:half]], 0))
    weight = np.full((half + 1,), 2.0, np.float32)
    weight[0] = weight[half] = 1.0
    cos_w = cos_b.astype(BF16).astype(np.float32) * weight[:, None]
    sin_w = sin_b.astype(BF16).astype(np.float32) * weight[:, None]
    last = np.concatenate([cos_w[:half], cos_w[half:], -sin_w[1:half]], 0).T / transform
    cos_l, sin_l = turn_table(np.arange(tok)[:, None], np.arange(tok)[None, :], tok)
    forward = np.block([[cos_l, -sin_l], [sin_l, cos_l]])
    backward = np.block([[cos_l, sin_l], [-sin_l, cos_l]])
    turn_cos, turn_sin = turn_table(kb[:, None], np.arange(tok)[None, :], transform)
    return (
        first.astype(BF16),
        forward.astype(BF16),
        backward.astype(BF16),
        last.astype(BF16),
        turn_cos[:half],
        turn_sin[:half],
        turn_cos[half:],
        turn_sin[half:],
    )


def featurized(rows, rim, taps):
    rows = rows.astype(F32)
    rim = rim.astype(F32)
    taps = taps.astype(F32)
    index = lax.broadcasted_iota(jnp.int32, rows.shape, 0)
    back1 = jnp.where(index == 0, rim[1:2], pltpu.roll(rows, 1, 0))
    back2 = pltpu.roll(rows, 2, 0)
    back2 = jnp.where(index == 0, rim[0:1], jnp.where(index == 1, rim[1:2], back2))
    return taps[0:1] * rows + taps[1:2] * back1 + taps[2:3] * back2


def gate_kernel(k_ref, v_ref, rk_ref, rv_ref, wk_ref, wv_ref, f_ref, send_ref, gated_ref):
    gated = featurized(k_ref[...], rk_ref[...], wk_ref[...]) * featurized(
        v_ref[...], rv_ref[...], wv_ref[...]
    )
    gated = gated.astype(BF16)
    gated_ref[...] = gated
    dests, twice, tok = send_ref.shape
    own = twice // 2
    send_ref[:, :own, :] = gated.T.reshape(dests, own, tok)
    send_ref[:, own:, :] = f_ref[...].T.reshape(dests, own, tok)


def gate(projected, rim, short_filter, long_filter, devices):
    tok, width = long_filter.shape
    own = width // devices
    steps = 8
    cols = width // steps
    peers = devices // steps

    def col(third):
        return lambda i: (0, i + third * steps)

    return pl.pallas_call(
        gate_kernel,
        grid=(steps,),
        in_specs=[
            pl.BlockSpec((tok, cols), col(1)),
            pl.BlockSpec((tok, cols), col(2)),
            pl.BlockSpec((rim.shape[0], cols), col(1)),
            pl.BlockSpec((rim.shape[0], cols), col(2)),
            pl.BlockSpec((short_filter.shape[0], cols), col(1)),
            pl.BlockSpec((short_filter.shape[0], cols), col(2)),
            pl.BlockSpec((tok, cols), lambda i: (0, i)),
        ],
        out_specs=[
            pl.BlockSpec((peers, 2 * own, tok), lambda i: (i, 0, 0)),
            pl.BlockSpec((tok, cols), lambda i: (0, i)),
        ],
        out_shape=[
            jax.ShapeDtypeStruct((devices, 2 * own, tok), BF16),
            jax.ShapeDtypeStruct((tok, width), BF16),
        ],
        name="gate",
    )(projected, projected, rim, rim, short_filter, short_filter, long_filter)


def dot(a, b):
    return jnp.dot(a, b, preferred_element_type=F32)


def spectral_kernel(
    z_ref, first_ref, fwd_ref, bwd_ref, last_ref, tc_ref, ts_ref, hc_ref, hs_ref, out_ref,
    rows_ref, spec_ref, half_ref, half_out_ref, prod_ref, back_ref, conv_ref,
):
    segments, both, tok = z_ref.shape
    own = both // 2
    pitch = rows_ref.shape[0] // segments
    out_pitch = conv_ref.shape[0] // segments
    piece = 16

    def widen(i, carry):
        for j in range(piece):
            b = i * piece + j
            rows_ref[pl.ds(b * pitch, both), :] = z_ref[b].astype(F32)
        return carry

    lax.fori_loop(0, segments // piece, widen, 0)

    top = 8
    index = lax.broadcasted_iota(jnp.int32, (top, tok), 0)

    def first_row(row, block):
        return jnp.concatenate([jnp.where(index == 0, row, block[:top]), block[top:]], 0)

    group, group2, group3, group4 = 16, 16, 16, 32

    run = 16

    def first_section(which, i, carry):
        start = i * group
        base = which * own + start
        cols = [
            rows_ref[pl.ds(base + j, segments, stride=pitch), :].astype(BF16)
            for j in range(group)
        ]
        out = dot(first_ref[...], jnp.concatenate(cols, 1))
        out = out.reshape(segments // top, 2, top, group * tok)
        tc, ts = tc_ref[...], ts_ref[...]
        for j in range(group):
            real = out[:, 0, :, j * tok : (j + 1) * tok].reshape(segments, tok)
            imag = out[:, 1, :, j * tok : (j + 1) * tok].reshape(segments, tok)
            half_ref[pl.ds(base + j, 1), :] = imag[0:1]
            imag = first_row(0.0, imag)
            both_parts = jnp.concatenate([real * tc + imag * ts, imag * tc - real * ts], 1)
            both_parts = both_parts.astype(BF16).reshape(segments // run, run, 2 * tok)
            spec_ref[start + j, :, which] = both_parts
        return carry

    for which in range(2):
        lax.fori_loop(0, own // group, functools.partial(first_section, which), 0)

    def product(sig, fil):
        sr, si, fr, fi = sig[:, :tok], sig[:, tok:], fil[:, :tok], fil[:, tok:]
        return jnp.concatenate(
            [(sr * fr - si * fi).astype(BF16), (sr * fi + si * fr).astype(BF16)], 1
        )

    half = half_ref[...]
    hc, hs = hc_ref[...], hs_ref[...]
    half = jnp.concatenate([(half * hc).astype(BF16), (-half * hs).astype(BF16)], 1)
    half = dot(half, fwd_ref[...])
    half = dot(product(half[:own], half[own:]), bwd_ref[...])
    half_out_ref[...] = half[:, :tok] * hc - half[:, tok:] * hs

    def multiply(i, carry):
        start = i * group2
        spec = spec_ref[pl.ds(start, group2)].reshape(group2 * 2 * segments, 2 * tok)
        spec = dot(spec, fwd_ref[...]).reshape(group2 * segments // run, 2, run, 2 * tok)
        sig = spec[:, 0].reshape(group2 * segments, 2 * tok)
        fil = spec[:, 1].reshape(group2 * segments, 2 * tok)
        prod_ref[pl.ds(start, group2)] = product(sig, fil).reshape(group2, segments, 2 * tok)
        return carry

    lax.fori_loop(0, own // group2, multiply, 0)

    def invert(i, carry):
        start = i * group3
        tc, ts = tc_ref[...], ts_ref[...]
        back = dot(
            prod_ref[pl.ds(start, group3)].reshape(group3 * segments, 2 * tok), bwd_ref[...]
        )
        for j in range(group3):
            br = back[j * segments : (j + 1) * segments, :tok]
            bi = back[j * segments : (j + 1) * segments, tok:]
            imag = first_row(half_out_ref[pl.ds(start + j, 1), :], bi * tc + br * ts)
            back_ref[start + j, :segments] = (br * tc - bi * ts).astype(BF16)
            back_ref[start + j, segments:] = imag.astype(BF16)
        return carry

    lax.fori_loop(0, own // group3, invert, 0)

    def finish(i, carry):
        start = i * group4
        stacked = jnp.concatenate([back_ref[start + j] for j in range(group4)], 1)
        conv = dot(last_ref[...], stacked)
        for j in range(group4):
            conv_ref[pl.ds(start + j, segments, stride=out_pitch), :] = conv[
                :, j * tok : (j + 1) * tok
            ]
        return carry

    lax.fori_loop(0, own // group4, finish, 0)

    def narrow(i, carry):
        for j in range(piece):
            b = i * piece + j
            out_ref[b] = conv_ref[pl.ds(b * out_pitch, own), :].astype(BF16)
        return carry

    lax.fori_loop(0, segments // piece, narrow, 0)


def spectral(received, consts):
    segments, both, tok = received.shape
    own = both // 2
    return pl.pallas_call(
        spectral_kernel,
        out_shape=jax.ShapeDtypeStruct((segments, own, tok), BF16),
        in_specs=[pl.BlockSpec(memory_space=pltpu.VMEM)] * 9,
        out_specs=pl.BlockSpec(memory_space=pltpu.VMEM),
        scratch_shapes=[
            pltpu.VMEM((segments * (both + PAD), tok), F32),
            pltpu.VMEM((own, segments // 16, 2, 16, 2 * tok), BF16),
            pltpu.VMEM((both, tok), F32),
            pltpu.VMEM((own, tok), F32),
            pltpu.VMEM((own, segments, 2 * tok), BF16),
            pltpu.VMEM((own, 2 * segments, tok), BF16),
            pltpu.VMEM((segments * (own + PAD), tok), F32),
        ],
        name="spectral",
    )(received, *consts)


def mix_kernel(c_ref, q_ref, s_ref, out_ref):
    peers, own, tok = c_ref.shape
    conv = c_ref[...].reshape(peers * own, tok).T.astype(F32)
    out_ref[...] = (q_ref[...] * (conv + s_ref[...])).astype(BF16)


def mix(conv, query, direct):
    devices, own, tok = conv.shape
    width = devices * own
    steps = 8
    cols = width // steps
    wide = pl.BlockSpec((tok, cols), lambda i: (0, i))
    return pl.pallas_call(
        mix_kernel,
        grid=(steps,),
        in_specs=[pl.BlockSpec((devices // steps, own, tok), lambda i: (i, 0, 0)), wide, wide],
        out_specs=wide,
        out_shape=jax.ShapeDtypeStruct((tok, width), BF16),
        name="mix",
    )(conv, query, direct)


def shards(projected, short_filter, long_filter, skip):
    devices = lax.axis_size(AXES)
    tok, width = long_filter.shape
    tap_count = short_filter.shape[0]
    rim_count = tap_count - 1
    consts = tables(devices, tok)
    rim = lax.ppermute(
        projected[tok - rim_count :], AXES, [(i, i + 1) for i in range(devices - 1)]
    )
    send, gated = gate(projected, rim, short_filter, long_filter, devices)
    received = lax.all_to_all(send, AXES, split_axis=0, concat_axis=0, tiled=True)
    extended = jnp.concatenate([rim[:, :width], projected[:, :width]], 0).astype(F32)
    query = jnp.zeros((tok, width), F32)
    for tap in range(tap_count):
        offset = rim_count - tap
        query = query + short_filter[tap, :width].astype(F32) * extended[offset : offset + tok]
    direct = skip[None, :] * gated.astype(F32)
    conv = spectral(received, consts)
    conv = lax.all_to_all(conv, AXES, split_axis=0, concat_axis=0, tiled=True)
    return mix(conv, query, direct)


def solution(mesh):
    in_specs = (P(AXES, None), P(), P(AXES, None), P())
    return jax.shard_map(
        shards, mesh=mesh, in_specs=in_specs, out_specs=P(AXES, None), check_vma=False
    )
```

```python
import functools
import math

import jax
import jax.numpy as jnp
import numpy as np
from jax import lax
from jax.experimental import pallas as pl
from jax.experimental.pallas import tpu as pltpu
from jax.sharding import PartitionSpec as P

AXES = ("outer", "inner")
F32 = jnp.float32
BF16 = jnp.bfloat16
PAD = 1


def turn_table(rows, cols, length):
    product = (np.asarray(rows, np.int64) * np.asarray(cols, np.int64)) % length
    angle = product.astype(np.float32) * np.float32(2.0 * math.pi / length)
    angle = angle.astype(np.float64)
    return np.cos(angle).astype(np.float32), np.sin(angle).astype(np.float32)


def paired(reals, imags):
    both = np.stack([reals.reshape(-1, 8, reals.shape[1]), imags.reshape(-1, 8, imags.shape[1])], 1)
    return both.reshape(-1, reals.shape[1])


def tables(segments, tok):
    half = segments
    blocks = 2 * segments
    transform = blocks * tok
    kb = np.arange(half + 1)
    cos_b, sin_b = turn_table(kb[:, None], np.arange(segments)[None, :], blocks)
    first = paired(cos_b[:half], np.concatenate([cos_b[half:], -sin_b[1:half]], 0))
    weight = np.full((half + 1,), 2.0, np.float32)
    weight[0] = weight[half] = 1.0
    cos_w = cos_b.astype(BF16).astype(np.float32) * weight[:, None]
    sin_w = sin_b.astype(BF16).astype(np.float32) * weight[:, None]
    last = np.concatenate([cos_w[:half], cos_w[half:], -sin_w[1:half]], 0).T / transform
    cos_l, sin_l = turn_table(np.arange(tok)[:, None], np.arange(tok)[None, :], tok)
    forward = np.block([[cos_l, -sin_l], [sin_l, cos_l]])
    backward = np.block([[cos_l, sin_l], [-sin_l, cos_l]])
    turn_cos, turn_sin = turn_table(kb[:, None], np.arange(tok)[None, :], transform)
    return (
        first.astype(BF16),
        forward.astype(BF16),
        backward.astype(BF16),
        last.astype(BF16),
        turn_cos[:half],
        turn_sin[:half],
        turn_cos[half:],
        turn_sin[half:],
    )


def featurized(rows, rim, taps):
    rows = rows.astype(F32)
    rim = rim.astype(F32)
    taps = taps.astype(F32)
    index = lax.broadcasted_iota(jnp.int32, rows.shape, 0)
    back1 = jnp.where(index == 0, rim[1:2], pltpu.roll(rows, 1, 0))
    back2 = pltpu.roll(rows, 2, 0)
    back2 = jnp.where(index == 0, rim[0:1], jnp.where(index == 1, rim[1:2], back2))
    return taps[0:1] * rows + taps[1:2] * back1 + taps[2:3] * back2


def gate_kernel(k_ref, v_ref, rk_ref, rv_ref, wk_ref, wv_ref, f_ref, send_ref, gated_ref):
    gated = featurized(k_ref[...], rk_ref[...], wk_ref[...]) * featurized(
        v_ref[...], rv_ref[...], wv_ref[...]
    )
    gated = gated.astype(BF16)
    gated_ref[...] = gated
    dests, twice, tok = send_ref.shape
    own = twice // 2
    send_ref[:, :own, :] = gated.T.reshape(dests, own, tok)
    send_ref[:, own:, :] = f_ref[...].T.reshape(dests, own, tok)


def gate(projected, rim, short_filter, long_filter, devices):
    tok, width = long_filter.shape
    own = width // devices
    steps = 8
    cols = width // steps
    peers = devices // steps

    def col(third):
        return lambda i: (0, i + third * steps)

    return pl.pallas_call(
        gate_kernel,
        grid=(steps,),
        in_specs=[
            pl.BlockSpec((tok, cols), col(1)),
            pl.BlockSpec((tok, cols), col(2)),
            pl.BlockSpec((rim.shape[0], cols), col(1)),
            pl.BlockSpec((rim.shape[0], cols), col(2)),
            pl.BlockSpec((short_filter.shape[0], cols), col(1)),
            pl.BlockSpec((short_filter.shape[0], cols), col(2)),
            pl.BlockSpec((tok, cols), lambda i: (0, i)),
        ],
        out_specs=[
            pl.BlockSpec((peers, 2 * own, tok), lambda i: (i, 0, 0)),
            pl.BlockSpec((tok, cols), lambda i: (0, i)),
        ],
        out_shape=[
            jax.ShapeDtypeStruct((devices, 2 * own, tok), BF16),
            jax.ShapeDtypeStruct((tok, width), BF16),
        ],
        name="gate",
    )(projected, projected, rim, rim, short_filter, short_filter, long_filter)


def dot(a, b):
    return jnp.dot(a, b, preferred_element_type=F32)


def spectral_kernel(
    z_ref, first_ref, fwd_ref, bwd_ref, last_ref, tc_ref, ts_ref, hc_ref, hs_ref, out_ref,
    rows_ref, spec_ref, half_ref, half_out_ref, prod_ref, back_ref, conv_ref,
):
    segments, both, tok = z_ref.shape
    own = both // 2
    pitch = rows_ref.shape[0] // segments
    out_pitch = conv_ref.shape[0] // segments
    piece = 16

    def widen(i, carry):
        for j in range(piece):
            b = i * piece + j
            rows_ref[pl.ds(b * pitch, both), :] = z_ref[b].astype(F32)
        return carry

    lax.fori_loop(0, segments // piece, widen, 0)

    top = 8
    index = lax.broadcasted_iota(jnp.int32, (top, tok), 0)

    def first_row(row, block):
        return jnp.concatenate([jnp.where(index == 0, row, block[:top]), block[top:]], 0)

    group, group2, group3, group4 = 16, 16, 16, 32

    run = 16

    def first_section(which, i, carry):
        start = i * group
        base = which * own + start
        cols = [
            rows_ref[pl.ds(base + j, segments, stride=pitch), :].astype(BF16)
            for j in range(group)
        ]
        out = dot(first_ref[...], jnp.concatenate(cols, 1))
        out = out.reshape(segments // top, 2, top, group * tok)
        tc, ts = tc_ref[...], ts_ref[...]
        for j in range(group):
            real = out[:, 0, :, j * tok : (j + 1) * tok].reshape(segments, tok)
            imag = out[:, 1, :, j * tok : (j + 1) * tok].reshape(segments, tok)
            half_ref[pl.ds(base + j, 1), :] = imag[0:1]
            imag = first_row(0.0, imag)
            both_parts = jnp.concatenate([real * tc + imag * ts, imag * tc - real * ts], 1)
            both_parts = both_parts.astype(BF16).reshape(segments // run, run, 2 * tok)
            spec_ref[start + j, :, which] = both_parts
        return carry

    for which in range(2):
        lax.fori_loop(0, own // group, functools.partial(first_section, which), 0)

    def product(sig, fil):
        sr, si, fr, fi = sig[:, :tok], sig[:, tok:], fil[:, :tok], fil[:, tok:]
        return jnp.concatenate(
            [(sr * fr - si * fi).astype(BF16), (sr * fi + si * fr).astype(BF16)], 1
        )

    half = half_ref[...]
    hc, hs = hc_ref[...], hs_ref[...]
    half = jnp.concatenate([(half * hc).astype(BF16), (-half * hs).astype(BF16)], 1)
    half = dot(half, fwd_ref[...])
    half = dot(product(half[:own], half[own:]), bwd_ref[...])
    half_out_ref[...] = half[:, :tok] * hc - half[:, tok:] * hs

    def multiply(i, carry):
        start = i * group2
        spec = spec_ref[pl.ds(start, group2)].reshape(group2 * 2 * segments, 2 * tok)
        spec = dot(spec, fwd_ref[...]).reshape(group2 * segments // run, 2, run, 2 * tok)
        sig = spec[:, 0].reshape(group2 * segments, 2 * tok)
        fil = spec[:, 1].reshape(group2 * segments, 2 * tok)
        prod_ref[pl.ds(start, group2)] = product(sig, fil).reshape(group2, segments, 2 * tok)
        return carry

    lax.fori_loop(0, own // group2, multiply, 0)

    def invert(i, carry):
        start = i * group3
        tc, ts = tc_ref[...], ts_ref[...]
        back = dot(
            prod_ref[pl.ds(start, group3)].reshape(group3 * segments, 2 * tok), bwd_ref[...]
        )
        for j in range(group3):
            br = back[j * segments : (j + 1) * segments, :tok]
            bi = back[j * segments : (j + 1) * segments, tok:]
            imag = first_row(half_out_ref[pl.ds(start + j, 1), :], bi * tc + br * ts)
            back_ref[start + j, :segments] = (br * tc - bi * ts).astype(BF16)
            back_ref[start + j, segments:] = imag.astype(BF16)
        return carry

    lax.fori_loop(0, own // group3, invert, 0)

    def finish(i, carry):
        start = i * group4
        stacked = jnp.concatenate([back_ref[start + j] for j in range(group4)], 1)
        conv = dot(last_ref[...], stacked)
        for j in range(group4):
            conv_ref[pl.ds(start + j, segments, stride=out_pitch), :] = conv[
                :, j * tok : (j + 1) * tok
            ]
        return carry

    lax.fori_loop(0, own // group4, finish, 0)

    def narrow(i, carry):
        for j in range(piece):
            b = i * piece + j
            out_ref[b] = conv_ref[pl.ds(b * out_pitch, own), :].astype(BF16)
        return carry

    lax.fori_loop(0, segments // piece, narrow, 0)


def spectral(received, consts):
    segments, both, tok = received.shape
    own = both // 2
    return pl.pallas_call(
        spectral_kernel,
        out_shape=pltpu.VMEM((segments, own, tok), BF16),
        in_specs=[pl.BlockSpec(memory_space=pltpu.VMEM)] * 9,
        out_specs=pl.BlockSpec(memory_space=pltpu.VMEM),
        scratch_shapes=[
            pltpu.VMEM((segments * (both + PAD), tok), F32),
            pltpu.VMEM((own, segments // 16, 2, 16, 2 * tok), BF16),
            pltpu.VMEM((both, tok), F32),
            pltpu.VMEM((own, tok), F32),
            pltpu.VMEM((own, segments, 2 * tok), BF16),
            pltpu.VMEM((own, 2 * segments, tok), BF16),
            pltpu.VMEM((segments * (own + PAD), tok), F32),
        ],
        compiler_params=pltpu.CompilerParams(vmem_limit_bytes=28 << 20),
        name="spectral",
    )(resident(received), *consts)


def mix_kernel(c_ref, q_ref, s_ref, out_ref, sem):
    peers, own, tok = c_ref.shape
    steps = 8
    peers = peers // steps
    cols = peers * own

    def run(buf_ref):
        for i in range(steps):
            conv = c_ref[i * peers : (i + 1) * peers].reshape(cols, tok).T.astype(F32)
            at = pl.ds(i * cols, cols)
            buf_ref[:, at] = (q_ref[:, at] * (conv + s_ref[:, at])).astype(BF16)
            pltpu.make_async_copy(buf_ref.at[:, at], out_ref.at[:, at], sem.at[i]).start()
        for i in range(steps):
            at = pl.ds(i * cols, cols)
            pltpu.make_async_copy(buf_ref.at[:, at], out_ref.at[:, at], sem.at[i]).wait()

    pl.run_scoped(run, pltpu.VMEM(out_ref.shape, BF16))


def resident(value):
    return pltpu.with_memory_space_constraint(value, pltpu.VMEM)


def mix(conv, query, direct):
    devices, own, tok = conv.shape
    return pl.pallas_call(
        mix_kernel,
        in_specs=[pl.BlockSpec(memory_space=pltpu.VMEM)] * 3,
        out_specs=pl.BlockSpec(memory_space=pl.ANY),
        out_shape=jax.ShapeDtypeStruct((tok, devices * own), BF16),
        scratch_shapes=[pltpu.SemaphoreType.DMA((8,))],
        compiler_params=pltpu.CompilerParams(vmem_limit_bytes=6 << 20),
        name="mix",
    )(resident(conv), resident(query), resident(direct))


def shards(projected, short_filter, long_filter, skip):
    devices = lax.axis_size(AXES)
    tok, width = long_filter.shape
    tap_count = short_filter.shape[0]
    rim_count = tap_count - 1
    consts = tables(devices, tok)
    rim = lax.ppermute(
        projected[tok - rim_count :], AXES, [(i, i + 1) for i in range(devices - 1)]
    )
    send, gated = gate(projected, rim, short_filter, long_filter, devices)
    received = lax.all_to_all(send, AXES, split_axis=0, concat_axis=0, tiled=True)
    extended = jnp.concatenate([rim[:, :width], projected[:, :width]], 0).astype(F32)
    query = jnp.zeros((tok, width), F32)
    for tap in range(tap_count):
        offset = rim_count - tap
        query = query + short_filter[tap, :width].astype(F32) * extended[offset : offset + tok]
    direct = skip[None, :] * gated.astype(F32)
    conv = spectral(received, consts)
    conv = lax.all_to_all(conv, AXES, split_axis=0, concat_axis=0, tiled=True)
    return mix(conv, query, direct)


def solution(mesh):
    in_specs = (P(AXES, None), P(), P(AXES, None), P())
    return jax.shard_map(
        shards, mesh=mesh, in_specs=in_specs, out_specs=P(AXES, None), check_vma=False
    )
```

```python
import functools
import math

import jax
import jax.numpy as jnp
import numpy as np
from jax import lax
from jax.experimental import pallas as pl
from jax.experimental.pallas import tpu as pltpu
from jax.sharding import PartitionSpec as P


AXES = ("outer", "inner")
F32 = jnp.float32
BF16 = jnp.bfloat16
PAD = 1


def turn_table(rows, cols, length):
    product = (np.asarray(rows, np.int64) * np.asarray(cols, np.int64)) % length
    angle = product.astype(np.float32) * np.float32(2.0 * math.pi / length)
    angle = angle.astype(np.float64)
    return np.cos(angle).astype(np.float32), np.sin(angle).astype(np.float32)


def paired(reals, imags):
    both = np.stack([reals.reshape(-1, 8, reals.shape[1]), imags.reshape(-1, 8, imags.shape[1])], 1)
    return both.reshape(-1, reals.shape[1])


def tables(segments, tok):
    half = segments
    blocks = 2 * segments
    transform = blocks * tok
    kb = np.arange(half + 1)
    cos_b, sin_b = turn_table(kb[:, None], np.arange(segments)[None, :], blocks)
    first = paired(cos_b[:half], np.concatenate([cos_b[half:], -sin_b[1:half]], 0))
    weight = np.full((half + 1,), 2.0, np.float32)
    weight[0] = weight[half] = 1.0
    cos_w = cos_b.astype(BF16).astype(np.float32) * weight[:, None]
    sin_w = sin_b.astype(BF16).astype(np.float32) * weight[:, None]
    last = np.concatenate([cos_w[:half], cos_w[half:], -sin_w[1:half]], 0).T / transform
    cos_l, sin_l = turn_table(np.arange(tok)[:, None], np.arange(tok)[None, :], tok)
    forward = np.block([[cos_l, -sin_l], [sin_l, cos_l]])
    backward = np.block([[cos_l, sin_l], [-sin_l, cos_l]])
    turn_cos, turn_sin = turn_table(kb[:, None], np.arange(tok)[None, :], transform)
    return (
        first.astype(BF16),
        forward.astype(BF16),
        backward.astype(BF16),
        last.astype(BF16),
        turn_cos[:half],
        turn_sin[:half],
        turn_cos[half:],
        turn_sin[half:],
    )


EXTRA = 8


def in_hbm(value):
    return pltpu.with_memory_space_constraint(value, pltpu.HBM)


def gate_kernel(p_ref, f_ref, t_ref, send_ref, w_ref, k_buf, v_buf, f_buf, out_buf, k_ext, v_ext, e_ext, sem, tap_sem):
    tok, width = f_ref.shape
    devices, _, _ = send_ref.shape
    own = width // devices
    steps = sem.shape[0]
    cols = width // steps
    peers = devices // steps

    def reads(i):
        at = pl.ds(i * cols, cols)
        return (
            pltpu.make_async_copy(
                p_ref.at[:, pl.ds(width + i * cols, cols)], k_buf.at[:, at], sem.at[i, 0]
            ),
            pltpu.make_async_copy(
                p_ref.at[:, pl.ds(2 * width + i * cols, cols)], v_buf.at[:, at], sem.at[i, 1]
            ),
            pltpu.make_async_copy(f_ref.at[:, at], f_buf.at[:, at], sem.at[i, 2]),
        )

    def write(i):
        at = pl.ds(i * peers, peers)
        return pltpu.make_async_copy(out_buf.at[at], send_ref.at[at], sem.at[i, 3])

    taps_read = pltpu.make_async_copy(t_ref, w_ref, tap_sem)
    taps_read.start()
    for i in range(steps):
        for copy in reads(i):
            copy.start()
    lead = 8
    lanes = k_ext.shape[2]
    for j in range(cols // lanes):
        k_ext[j, :lead] = jnp.zeros((lead, lanes), F32)
        v_ext[j, :lead] = jnp.zeros((lead, lanes), F32)
    taps_read.wait()
    for i in range(steps):
        for copy in reads(i):
            copy.wait()
        for j in range(cols // lanes):
            start = i * cols + j * lanes
            at = slice(start, start + lanes)

            def featurized(buf, ext, base):
                taps = w_ref[:, base + start : base + start + lanes].astype(F32)
                ext[j, lead:] = buf[:, at].astype(F32)
                return (
                    taps[0:1] * ext[j, lead : lead + tok]
                    + taps[1:2] * ext[j, pl.ds(lead - 1, tok)]
                    + taps[2:3] * ext[j, pl.ds(lead - 2, tok)]
                )

            gated = featurized(k_buf, k_ext, width) * featurized(v_buf, v_ext, 2 * width)
            near = lanes // own
            to = slice(start // own, start // own + near)
            out_buf[to, :own] = gated.astype(BF16).T.reshape(near, own, tok)
            out_buf[to, own : 2 * own] = f_buf[:, at].T.reshape(near, own, tok)
            e_ext[0:2] = k_ext[j, lead : lead + 2]
            e_ext[2:4] = v_ext[j, lead : lead + 2]
            e_ext[4:6] = k_ext[j, lead + tok - 2 : lead + tok]
            e_ext[6:8] = v_ext[j, lead + tok - 2 : lead + tok]
            tile = e_ext[...]
            for k in range(near):
                turned = pltpu.roll(tile, lanes - k * own, 1) if k else tile
                out_buf[start // own + k, 2 * own :] = turned.astype(BF16)
        write(i).start()
    for i in range(steps):
        write(i).wait()


def gate(projected, short_filter, long_filter, devices):
    tok, width = long_filter.shape
    own = width // devices
    steps = 8
    cols = width // steps
    rows = 2 * own + EXTRA
    return pl.pallas_call(
        gate_kernel,
        in_specs=[
            pl.BlockSpec(memory_space=pltpu.HBM),
            pl.BlockSpec(memory_space=pltpu.HBM),
            pl.BlockSpec(memory_space=pltpu.HBM),
        ],
        out_specs=pl.BlockSpec(memory_space=pltpu.HBM),
        out_shape=pltpu.HBM((devices, rows, tok), BF16),
        scratch_shapes=[
            pltpu.VMEM(short_filter.shape, BF16),
            pltpu.VMEM((tok, width), BF16),
            pltpu.VMEM((tok, width), BF16),
            pltpu.VMEM((tok, width), BF16),
            pltpu.VMEM((devices, rows, tok), BF16),
            pltpu.VMEM((cols // 128, tok + 8, 128), F32),
            pltpu.VMEM((cols // 128, tok + 8, 128), F32),
            pltpu.VMEM((EXTRA, 128), F32),
            pltpu.SemaphoreType.DMA((steps, 4)),
            pltpu.SemaphoreType.DMA(()),
        ],
        compiler_params=pltpu.CompilerParams(vmem_limit_bytes=16 << 20),
        name="gate",
    )(in_hbm(projected), in_hbm(long_filter), in_hbm(short_filter))


def dot(a, b):
    return jnp.dot(a, b, preferred_element_type=F32)


def spectral_kernel(
    z_ref, taps_ref, first_ref, fwd_ref, bwd_ref, last_ref, tc_ref, ts_ref, hc_ref, hs_ref,
    out_ref, rows_ref, fix_ref, spec_ref, half_ref, half_out_ref, prod_ref, back_ref, conv_ref, block_ref, sem,
):
    segments, rows, tok = z_ref.shape
    both = rows - EXTRA
    own = both // 2
    pitch = rows_ref.shape[0] // (segments + 1)
    out_pitch = conv_ref.shape[0] // segments
    piece = 16

    def widen(i, carry):
        for j in range(piece):
            b = i * piece + j
            rows_ref[pl.ds((b + 1) * pitch, rows), :] = z_ref[b].astype(F32)
        return carry

    lax.fori_loop(0, segments // piece, widen, 0)

    rows_ref[both:rows, :] = jnp.zeros((EXTRA, tok), F32)

    def sent(row, before):
        return rows_ref[pl.ds(both + row + (1 - before) * pitch, segments, stride=pitch), :]

    def edge(tap, at):
        now0, now1 = sent(at, 0), sent(at + 1, 0)
        ago2, ago1 = sent(at + 4, 1), sent(at + 5, 1)
        taps = [taps_ref[tap + n : tap + n + 1, :] for n in range(3)]
        return (
            taps[0] * now0 + taps[1] * ago1 + taps[2] * ago2,
            taps[0] * now1 + taps[1] * now0 + taps[2] * ago1,
        )

    key0, key1 = edge(0, 0)
    value0, value1 = edge(3, 2)
    gated0 = key0 * value0
    gated1 = pltpu.roll(key1 * value1, 1, 1)
    lane = lax.broadcasted_iota(jnp.int32, (segments, tok), 1)
    fix_ref[0] = jnp.where(lane % 2 == 0, gated0, gated1)
    fix_ref[1] = jnp.where(lane % 2 == 1, gated0, gated1)

    top = 8
    index = lax.broadcasted_iota(jnp.int32, (top, tok), 0)

    def first_row(row, block):
        return jnp.concatenate([jnp.where(index == 0, row, block[:top]), block[top:]], 0)

    group, group2, group3, group4 = 16, 16, 16, 32

    run = 16

    def first_section(which, i, carry):
        start = i * group
        base = which * own + start
        cols = []
        for j in range(group):
            col = rows_ref[pl.ds(base + j + pitch, segments, stride=pitch), :]
            if which == 0:
                fixed = pltpu.roll(fix_ref[j % 2], (tok - start - j) % tok, 1)
                col = jnp.where(lane < 2, fixed, col)
            cols.append(col.astype(BF16))
        out = dot(first_ref[...], jnp.concatenate(cols, 1))
        out = out.reshape(segments // top, 2, top, group * tok)
        tc, ts = tc_ref[...], ts_ref[...]
        for j in range(group):
            real = out[:, 0, :, j * tok : (j + 1) * tok].reshape(segments, tok)
            imag = out[:, 1, :, j * tok : (j + 1) * tok].reshape(segments, tok)
            half_ref[pl.ds(base + j, 1), :] = imag[0:1]
            imag = first_row(0.0, imag)
            both_parts = jnp.concatenate([real * tc + imag * ts, imag * tc - real * ts], 1)
            both_parts = both_parts.astype(BF16).reshape(segments // run, run, 2 * tok)
            spec_ref[start + j, :, which] = both_parts
        return carry

    for which in range(2):
        lax.fori_loop(0, own // group, functools.partial(first_section, which), 0)

    def product(sig, fil):
        sr, si, fr, fi = sig[:, :tok], sig[:, tok:], fil[:, :tok], fil[:, tok:]
        return jnp.concatenate(
            [(sr * fr - si * fi).astype(BF16), (sr * fi + si * fr).astype(BF16)], 1
        )

    half = half_ref[...]
    hc, hs = hc_ref[...], hs_ref[...]
    half = jnp.concatenate([(half * hc).astype(BF16), (-half * hs).astype(BF16)], 1)
    half = dot(half, fwd_ref[...])
    half = dot(product(half[:own], half[own:]), bwd_ref[...])
    half_out_ref[...] = half[:, :tok] * hc - half[:, tok:] * hs

    def multiply(i, carry):
        start = i * group2
        spec = spec_ref[pl.ds(start, group2)].reshape(group2 * 2 * segments, 2 * tok)
        spec = dot(spec, fwd_ref[...]).reshape(group2 * segments // run, 2, run, 2 * tok)
        sig = spec[:, 0].reshape(group2 * segments, 2 * tok)
        fil = spec[:, 1].reshape(group2 * segments, 2 * tok)
        prod_ref[pl.ds(start, group2)] = product(sig, fil).reshape(group2, segments, 2 * tok)
        return carry

    lax.fori_loop(0, own // group2, multiply, 0)

    def invert(i, carry):
        start = i * group3
        tc, ts = tc_ref[...], ts_ref[...]
        back = dot(
            prod_ref[pl.ds(start, group3)].reshape(group3 * segments, 2 * tok), bwd_ref[...]
        )
        for j in range(group3):
            br = back[j * segments : (j + 1) * segments, :tok]
            bi = back[j * segments : (j + 1) * segments, tok:]
            imag = first_row(half_out_ref[pl.ds(start + j, 1), :], bi * tc + br * ts)
            back_ref[start + j, :segments] = (br * tc - bi * ts).astype(BF16)
            back_ref[start + j, segments:] = imag.astype(BF16)
        return carry

    lax.fori_loop(0, own // group3, invert, 0)

    def finish(i, carry):
        start = i * group4
        stacked = jnp.concatenate([back_ref[start + j] for j in range(group4)], 1)
        conv = dot(last_ref[...], stacked)
        for j in range(group4):
            conv_ref[pl.ds(start + j, segments, stride=out_pitch), :] = conv[
                :, j * tok : (j + 1) * tok
            ]
        return carry

    lax.fori_loop(0, own // group4, finish, 0)

    def write(i):
        at = pl.ds(i * piece, piece)
        return pltpu.make_async_copy(block_ref.at[at], out_ref.at[at], sem.at[i])

    for i in range(segments // piece):
        for b in range(i * piece, (i + 1) * piece):
            block_ref[b] = conv_ref[b * out_pitch : b * out_pitch + own, :].astype(BF16)
        write(i).start()
    for i in range(segments // piece):
        write(i).wait()


def spectral(received, taps, consts):
    segments, rows, tok = received.shape
    both = rows - EXTRA
    own = both // 2
    return pl.pallas_call(
        spectral_kernel,
        out_shape=pltpu.HBM((segments, own, tok), BF16),
        in_specs=[pl.BlockSpec(memory_space=pltpu.VMEM)] * 10,
        out_specs=pl.BlockSpec(memory_space=pltpu.HBM),
        scratch_shapes=[
            pltpu.VMEM(((segments + 1) * (rows + PAD), tok), F32),
            pltpu.VMEM((2, segments, tok), F32),
            pltpu.VMEM((own, segments // 16, 2, 16, 2 * tok), BF16),
            pltpu.VMEM((both, tok), F32),
            pltpu.VMEM((own, tok), F32),
            pltpu.VMEM((own, segments, 2 * tok), BF16),
            pltpu.VMEM((own, 2 * segments, tok), BF16),
            pltpu.VMEM((segments * (own + PAD), tok), F32),
            pltpu.VMEM((segments, own, tok), BF16),
            pltpu.SemaphoreType.DMA((segments // 16,)),
        ],
        compiler_params=pltpu.CompilerParams(vmem_limit_bytes=28 << 20),
        name="spectral",
    )(resident(received), taps, *consts)


def mix_kernel(c_ref, q_ref, skip_ref, g_ref, out_ref, g_buf, buf_ref, sem):
    peers, own, tok = c_ref.shape
    steps = sem.shape[0]
    peers = peers // steps
    cols = peers * own

    def read(i):
        at = pl.ds(i * cols, cols)
        return pltpu.make_async_copy(g_ref.at[:, at], g_buf.at[:, at], sem.at[i, 0])

    def write(i):
        at = pl.ds(i * cols, cols)
        return pltpu.make_async_copy(buf_ref.at[:, at], out_ref.at[:, at], sem.at[i, 1])

    for i in range(steps):
        read(i).start()
    for i in range(steps):
        at = slice(i * cols, (i + 1) * cols)
        conv = c_ref[i * peers : (i + 1) * peers].reshape(cols, tok).T.astype(F32)
        read(i).wait()
        direct = skip_ref[:, at] * g_buf[:, at].astype(F32)
        buf_ref[:, at] = (q_ref[:, at] * (conv + direct)).astype(BF16)
        write(i).start()
    for i in range(steps):
        write(i).wait()


def resident(value):
    return pltpu.with_memory_space_constraint(value, pltpu.VMEM)


def mix(conv, query, skip, gated):
    devices, own, tok = conv.shape
    width = devices * own
    steps = 8
    return pl.pallas_call(
        mix_kernel,
        in_specs=[pl.BlockSpec(memory_space=pltpu.VMEM)] * 3
        + [pl.BlockSpec(memory_space=pltpu.HBM)],
        out_specs=pl.BlockSpec(memory_space=pltpu.HBM),
        out_shape=jax.ShapeDtypeStruct((tok, width), BF16),
        scratch_shapes=[
            pltpu.VMEM((tok, width), BF16),
            pltpu.VMEM((tok, width), BF16),
            pltpu.SemaphoreType.DMA((steps, 2)),
        ],
        compiler_params=pltpu.CompilerParams(vmem_limit_bytes=6 << 20),
        name="mix",
    )(resident(conv), resident(query), resident(skip), in_hbm(gated))


def side_kernel(q_ref, k_ref, v_ref, rq_ref, rk_ref, rv_ref, wq_ref, wk_ref, wv_ref,
                query_ref, gated_ref):
    def featurized(rows_ref, rim_ref, taps_ref):
        rows = rows_ref[...].astype(F32)
        rim = rim_ref[...].astype(F32)
        taps = taps_ref[...].astype(F32)
        index = lax.broadcasted_iota(jnp.int32, rows.shape, 0)
        back1 = jnp.where(index == 0, rim[1:2], pltpu.roll(rows, 1, 0))
        back2 = pltpu.roll(rows, 2, 0)
        back2 = jnp.where(index == 0, rim[0:1], jnp.where(index == 1, rim[1:2], back2))
        return taps[0:1] * rows + taps[1:2] * back1 + taps[2:3] * back2

    query_ref[...] = featurized(q_ref, rq_ref, wq_ref)
    gated = featurized(k_ref, rk_ref, wk_ref) * featurized(v_ref, rv_ref, wv_ref)
    gated_ref[...] = gated.astype(BF16)


def side(projected, rim, short_filter):
    tok = projected.shape[0]
    width = projected.shape[1] // 3
    steps = 8
    cols = width // steps

    def thirds(rows):
        return [
            pl.BlockSpec((rows, cols), functools.partial(lambda third, i: (0, i + third * steps), t))
            for t in range(3)
        ]

    wide = pl.BlockSpec((tok, cols), lambda i: (0, i))
    return pl.pallas_call(
        side_kernel,
        grid=(steps,),
        in_specs=thirds(tok)
        + thirds(rim.shape[0])
        + thirds(short_filter.shape[0]),
        out_specs=[wide, wide],
        out_shape=[
            jax.ShapeDtypeStruct((tok, width), F32),
            pltpu.HBM((tok, width), BF16),
        ],
        compiler_params=pltpu.CompilerParams(vmem_limit_bytes=8 << 20),
        name="side",
    )(*[in_hbm(projected)] * 3, *[rim] * 3, *[short_filter] * 3)


def shards(projected, short_filter, long_filter, skip):
    devices = lax.axis_size(AXES)
    tok, width = long_filter.shape
    own = width // devices
    tap_count = short_filter.shape[0]
    rim_count = tap_count - 1
    consts = tables(devices, tok)
    position = lax.axis_index(AXES)
    taps = jnp.concatenate(
        [
            lax.dynamic_slice_in_dim(short_filter, third * width + position * own, own, 1)
            for third in (1, 2)
        ],
        0,
    ).astype(F32)
    taps = jnp.pad(taps, ((0, 8 - 2 * tap_count), (0, tok - own)))
    send = gate(projected, short_filter, long_filter, devices)
    received = lax.all_to_all(send, AXES, split_axis=0, concat_axis=0, tiled=True)
    rim = lax.ppermute(projected[tok - rim_count :], AXES, [(i, i + 1) for i in range(devices - 1)])
    query, gated = side(projected, rim, short_filter)
    conv = spectral(received, taps, consts)
    conv = lax.all_to_all(conv, AXES, split_axis=0, concat_axis=0, tiled=True)
    return mix(conv, query, skip[None, :], gated)


def solution(mesh):
    in_specs = (P(AXES, None), P(), P(AXES, None), P())
    return jax.shard_map(
        shards, mesh=mesh, in_specs=in_specs, out_specs=P(AXES, None), check_vma=False
    )
```

```python
import functools
import math

import jax
import jax.numpy as jnp
import numpy as np
from jax import lax
from jax.experimental import pallas as pl
from jax.experimental.pallas import tpu as pltpu
from jax.sharding import PartitionSpec as P


AXES = ("outer", "inner")
F32 = jnp.float32
BF16 = jnp.bfloat16
PAD = 1


def turn_table(rows, cols, length):
    product = (np.asarray(rows, np.int64) * np.asarray(cols, np.int64)) % length
    angle = product.astype(np.float32) * np.float32(2.0 * math.pi / length)
    angle = angle.astype(np.float64)
    return np.cos(angle).astype(np.float32), np.sin(angle).astype(np.float32)


def paired(reals, imags):
    both = np.stack([reals.reshape(-1, 8, reals.shape[1]), imags.reshape(-1, 8, imags.shape[1])], 1)
    return both.reshape(-1, reals.shape[1])


def tables(segments, tok):
    half = segments
    blocks = 2 * segments
    transform = blocks * tok
    kb = np.arange(half + 1)
    cos_b, sin_b = turn_table(kb[:, None], np.arange(segments)[None, :], blocks)
    first = paired(cos_b[:half], np.concatenate([cos_b[half:], -sin_b[1:half]], 0))
    weight = np.full((half + 1,), 2.0, np.float32)
    weight[0] = weight[half] = 1.0
    cos_w = cos_b.astype(BF16).astype(np.float32) * weight[:, None]
    sin_w = sin_b.astype(BF16).astype(np.float32) * weight[:, None]
    last = np.concatenate([cos_w[:half], cos_w[half:], -sin_w[1:half]], 0).T / transform
    cos_l, sin_l = turn_table(np.arange(tok)[:, None], np.arange(tok)[None, :], tok)
    forward = np.block([[cos_l, -sin_l], [sin_l, cos_l]])
    backward = np.block([[cos_l, sin_l], [-sin_l, cos_l]])
    turn_cos, turn_sin = turn_table(kb[:, None], np.arange(tok)[None, :], transform)
    return (
        first.astype(BF16),
        forward.astype(BF16),
        backward.astype(BF16),
        last.astype(BF16),
        turn_cos[:half],
        turn_sin[:half],
        turn_cos[half:],
        turn_sin[half:],
    )


EXTRA = 8


def in_hbm(value):
    return pltpu.with_memory_space_constraint(value, pltpu.HBM)


def gate_kernel(p_ref, f_ref, t_ref, send_ref, w_ref, k_buf, v_buf, f_buf, out_buf, k_ext, v_ext, e_ext, sem, tap_sem):
    tok, width = f_ref.shape
    devices, _, _ = send_ref.shape
    own = width // devices
    steps = sem.shape[0]
    cols = width // steps
    peers = devices // steps

    def reads(i):
        at = pl.ds(i * cols, cols)
        return (
            pltpu.make_async_copy(
                p_ref.at[:, pl.ds(width + i * cols, cols)], k_buf.at[:, at], sem.at[i, 0]
            ),
            pltpu.make_async_copy(
                p_ref.at[:, pl.ds(2 * width + i * cols, cols)], v_buf.at[:, at], sem.at[i, 1]
            ),
            pltpu.make_async_copy(f_ref.at[:, at], f_buf.at[:, at], sem.at[i, 2]),
        )

    def write(i):
        at = pl.ds(i * peers, peers)
        return pltpu.make_async_copy(out_buf.at[at], send_ref.at[at], sem.at[i, 3])

    taps_read = pltpu.make_async_copy(t_ref, w_ref, tap_sem)
    taps_read.start()
    for i in range(steps):
        for copy in reads(i):
            copy.start()
    lead = 8
    lanes = k_ext.shape[2]
    for j in range(cols // lanes):
        k_ext[j, :lead] = jnp.zeros((lead, lanes), F32)
        v_ext[j, :lead] = jnp.zeros((lead, lanes), F32)
    taps_read.wait()
    for i in range(steps):
        for copy in reads(i):
            copy.wait()
        for j in range(cols // lanes):
            start = i * cols + j * lanes
            at = slice(start, start + lanes)

            def featurized(buf, ext, base):
                taps = w_ref[:, base + start : base + start + lanes].astype(F32)
                ext[j, lead:] = buf[:, at].astype(F32)
                return (
                    taps[0:1] * ext[j, lead : lead + tok]
                    + taps[1:2] * ext[j, pl.ds(lead - 1, tok)]
                    + taps[2:3] * ext[j, pl.ds(lead - 2, tok)]
                )

            gated = featurized(k_buf, k_ext, width) * featurized(v_buf, v_ext, 2 * width)
            near = lanes // own
            to = slice(start // own, start // own + near)
            out_buf[to, :own] = gated.astype(BF16).T.reshape(near, own, tok)
            out_buf[to, own : 2 * own] = f_buf[:, at].T.reshape(near, own, tok)
            e_ext[0:2] = k_ext[j, lead : lead + 2]
            e_ext[2:4] = v_ext[j, lead : lead + 2]
            e_ext[4:6] = k_ext[j, lead + tok - 2 : lead + tok]
            e_ext[6:8] = v_ext[j, lead + tok - 2 : lead + tok]
            tile = e_ext[...]
            for k in range(near):
                turned = pltpu.roll(tile, lanes - k * own, 1) if k else tile
                out_buf[start // own + k, 2 * own :] = turned.astype(BF16)
        write(i).start()
    for i in range(steps):
        write(i).wait()


def gate(projected, short_filter, long_filter, devices):
    tok, width = long_filter.shape
    own = width // devices
    steps = 8
    cols = width // steps
    rows = 2 * own + EXTRA
    return pl.pallas_call(
        gate_kernel,
        in_specs=[
            pl.BlockSpec(memory_space=pltpu.HBM),
            pl.BlockSpec(memory_space=pltpu.HBM),
            pl.BlockSpec(memory_space=pltpu.HBM),
        ],
        out_specs=pl.BlockSpec(memory_space=pltpu.HBM),
        out_shape=pltpu.HBM((devices, rows, tok), BF16),
        scratch_shapes=[
            pltpu.VMEM(short_filter.shape, BF16),
            pltpu.VMEM((tok, width), BF16),
            pltpu.VMEM((tok, width), BF16),
            pltpu.VMEM((tok, width), BF16),
            pltpu.VMEM((devices, rows, tok), BF16),
            pltpu.VMEM((cols // 128, tok + 8, 128), F32),
            pltpu.VMEM((cols // 128, tok + 8, 128), F32),
            pltpu.VMEM((EXTRA, 128), F32),
            pltpu.SemaphoreType.DMA((steps, 4)),
            pltpu.SemaphoreType.DMA(()),
        ],
        compiler_params=pltpu.CompilerParams(vmem_limit_bytes=16 << 20),
        name="gate",
    )(in_hbm(projected), in_hbm(long_filter), in_hbm(short_filter))


def dot(a, b):
    return jnp.dot(a, b, preferred_element_type=F32)


def spectral_kernel(
    z_ref, taps_ref, first_ref, fwd_ref, bwd_ref, last_ref, tc_ref, ts_ref, hc_ref, hs_ref,
    out_ref, rows_ref, fix_ref, spec_ref, half_ref, half_out_ref, prod_ref, back_ref, conv_ref, block_ref, sem,
):
    segments, rows, tok = z_ref.shape
    both = rows - EXTRA
    own = both // 2
    pitch = rows_ref.shape[0] // (segments + 1)
    out_pitch = conv_ref.shape[0] // segments
    piece = 16

    def widen(i, carry):
        for j in range(piece):
            b = i * piece + j
            rows_ref[pl.ds((b + 1) * pitch, rows), :] = z_ref[b].astype(F32)
        return carry

    lax.fori_loop(0, segments // piece, widen, 0)

    rows_ref[both:rows, :] = jnp.zeros((EXTRA, tok), F32)

    def sent(row, before):
        return rows_ref[pl.ds(both + row + (1 - before) * pitch, segments, stride=pitch), :]

    def edge(tap, at):
        now0, now1 = sent(at, 0), sent(at + 1, 0)
        ago2, ago1 = sent(at + 4, 1), sent(at + 5, 1)
        taps = [taps_ref[tap + n : tap + n + 1, :] for n in range(3)]
        return (
            taps[0] * now0 + taps[1] * ago1 + taps[2] * ago2,
            taps[0] * now1 + taps[1] * now0 + taps[2] * ago1,
        )

    key0, key1 = edge(0, 0)
    value0, value1 = edge(3, 2)
    gated0 = key0 * value0
    gated1 = pltpu.roll(key1 * value1, 1, 1)
    lane = lax.broadcasted_iota(jnp.int32, (segments, tok), 1)
    fix_ref[0] = jnp.where(lane % 2 == 0, gated0, gated1)
    fix_ref[1] = jnp.where(lane % 2 == 1, gated0, gated1)

    top = 8
    index = lax.broadcasted_iota(jnp.int32, (top, tok), 0)

    def first_row(row, block):
        return jnp.concatenate([jnp.where(index == 0, row, block[:top]), block[top:]], 0)

    group, group2, group3, group4 = 16, 16, 16, 32

    run = 16

    def first_section(which, i, carry):
        start = i * group
        base = which * own + start
        cols = []
        for j in range(group):
            col = rows_ref[pl.ds(base + j + pitch, segments, stride=pitch), :]
            if which == 0:
                fixed = pltpu.roll(fix_ref[j % 2], (tok - start - j) % tok, 1)
                col = jnp.where(lane < 2, fixed, col)
            cols.append(col.astype(BF16))
        out = dot(first_ref[...], jnp.concatenate(cols, 1))
        out = out.reshape(segments // top, 2, top, group * tok)
        tc, ts = tc_ref[...], ts_ref[...]
        for j in range(group):
            real = out[:, 0, :, j * tok : (j + 1) * tok].reshape(segments, tok)
            imag = out[:, 1, :, j * tok : (j + 1) * tok].reshape(segments, tok)
            half_ref[pl.ds(base + j, 1), :] = imag[0:1]
            imag = first_row(0.0, imag)
            both_parts = jnp.concatenate([real * tc + imag * ts, imag * tc - real * ts], 1)
            both_parts = both_parts.astype(BF16).reshape(segments // run, run, 2 * tok)
            spec_ref[start + j, :, which] = both_parts
        return carry

    for which in range(2):
        lax.fori_loop(0, own // group, functools.partial(first_section, which), 0)

    def product(sig, fil):
        sr, si, fr, fi = sig[:, :tok], sig[:, tok:], fil[:, :tok], fil[:, tok:]
        return jnp.concatenate(
            [(sr * fr - si * fi).astype(BF16), (sr * fi + si * fr).astype(BF16)], 1
        )

    half = half_ref[...]
    hc, hs = hc_ref[...], hs_ref[...]
    half = jnp.concatenate([(half * hc).astype(BF16), (-half * hs).astype(BF16)], 1)
    half = dot(half, fwd_ref[...])
    half = dot(product(half[:own], half[own:]), bwd_ref[...])
    half_out_ref[...] = half[:, :tok] * hc - half[:, tok:] * hs

    def multiply(i, carry):
        start = i * group2
        spec = spec_ref[pl.ds(start, group2)].reshape(group2 * 2 * segments, 2 * tok)
        spec = dot(spec, fwd_ref[...]).reshape(group2 * segments // run, 2, run, 2 * tok)
        sig = spec[:, 0].reshape(group2 * segments, 2 * tok)
        fil = spec[:, 1].reshape(group2 * segments, 2 * tok)
        prod_ref[pl.ds(start, group2)] = product(sig, fil).reshape(group2, segments, 2 * tok)
        return carry

    lax.fori_loop(0, own // group2, multiply, 0)

    def invert(i, carry):
        start = i * group3
        tc, ts = tc_ref[...], ts_ref[...]
        back = dot(
            prod_ref[pl.ds(start, group3)].reshape(group3 * segments, 2 * tok), bwd_ref[...]
        )
        for j in range(group3):
            br = back[j * segments : (j + 1) * segments, :tok]
            bi = back[j * segments : (j + 1) * segments, tok:]
            imag = first_row(half_out_ref[pl.ds(start + j, 1), :], bi * tc + br * ts)
            back_ref[start + j, :segments] = (br * tc - bi * ts).astype(BF16)
            back_ref[start + j, segments:] = imag.astype(BF16)
        return carry

    lax.fori_loop(0, own // group3, invert, 0)

    def finish(i, carry):
        start = i * group4
        stacked = jnp.concatenate([back_ref[start + j] for j in range(group4)], 1)
        conv = dot(last_ref[...], stacked)
        for j in range(group4):
            conv_ref[pl.ds(start + j, segments, stride=out_pitch), :] = conv[
                :, j * tok : (j + 1) * tok
            ]
        return carry

    lax.fori_loop(0, own // group4, finish, 0)

    def write(i):
        at = pl.ds(i * piece, piece)
        return pltpu.make_async_copy(block_ref.at[at], out_ref.at[at], sem.at[i])

    for i in range(segments // piece):
        for b in range(i * piece, (i + 1) * piece):
            block_ref[b] = conv_ref[b * out_pitch : b * out_pitch + own, :].astype(BF16)
        write(i).start()
    for i in range(segments // piece):
        write(i).wait()


def spectral(received, taps, consts):
    segments, rows, tok = received.shape
    both = rows - EXTRA
    own = both // 2
    return pl.pallas_call(
        spectral_kernel,
        out_shape=pltpu.HBM((segments, own, tok), BF16),
        in_specs=[pl.BlockSpec(memory_space=pltpu.VMEM)] * 10,
        out_specs=pl.BlockSpec(memory_space=pltpu.HBM),
        scratch_shapes=[
            pltpu.VMEM(((segments + 1) * (rows + PAD), tok), F32),
            pltpu.VMEM((2, segments, tok), F32),
            pltpu.VMEM((own, segments // 16, 2, 16, 2 * tok), BF16),
            pltpu.VMEM((both, tok), F32),
            pltpu.VMEM((own, tok), F32),
            pltpu.VMEM((own, segments, 2 * tok), BF16),
            pltpu.VMEM((own, 2 * segments, tok), BF16),
            pltpu.VMEM((segments * (own + PAD), tok), F32),
            pltpu.VMEM((segments, own, tok), BF16),
            pltpu.SemaphoreType.DMA((segments // 16,)),
        ],
        compiler_params=pltpu.CompilerParams(vmem_limit_bytes=28 << 20),
        name="spectral",
    )(resident(received), taps, *consts)


def mix_kernel(c_ref, q_ref, skip_ref, g_ref, out_ref, g_buf, buf_ref, sem):
    peers, own, tok = c_ref.shape
    steps = sem.shape[0]
    peers = peers // steps
    cols = peers * own
    near = 128 // own

    def read(i):
        at = pl.ds(i * cols, cols)
        return pltpu.make_async_copy(g_ref.at[:, at], g_buf.at[:, at], sem.at[i, 0])

    def write(i):
        at = pl.ds(i * cols, cols)
        return pltpu.make_async_copy(buf_ref.at[:, at], out_ref.at[:, at], sem.at[i, 1])

    for i in range(steps):
        read(i).start()
    for i in range(steps):
        read(i).wait()
        for j in range(i * peers, (i + 1) * peers, near):
            at = slice(j * own, (j + near) * own)
            conv = c_ref[j : j + near].reshape(near * own, tok).T.astype(F32)
            direct = skip_ref[:, at] * g_buf[:, at].astype(F32)
            buf_ref[:, at] = (q_ref[:, at] * (conv + direct)).astype(BF16)
        write(i).start()
    for i in range(steps):
        write(i).wait()


def resident(value):
    return pltpu.with_memory_space_constraint(value, pltpu.VMEM)


def mix(conv, query, skip, gated):
    devices, own, tok = conv.shape
    width = devices * own
    steps = 8
    return pl.pallas_call(
        mix_kernel,
        in_specs=[pl.BlockSpec(memory_space=pltpu.VMEM)] * 3
        + [pl.BlockSpec(memory_space=pltpu.HBM)],
        out_specs=pl.BlockSpec(memory_space=pltpu.HBM),
        out_shape=jax.ShapeDtypeStruct((tok, width), BF16),
        scratch_shapes=[
            pltpu.VMEM((tok, width), BF16),
            pltpu.VMEM((tok, width), BF16),
            pltpu.SemaphoreType.DMA((steps, 2)),
        ],
        compiler_params=pltpu.CompilerParams(vmem_limit_bytes=6 << 20),
        name="mix",
    )(resident(conv), resident(query), resident(skip), in_hbm(gated))


def side_kernel(q_ref, k_ref, v_ref, rq_ref, rk_ref, rv_ref, wq_ref, wk_ref, wv_ref,
                query_ref, gated_ref):
    def featurized(rows_ref, rim_ref, taps_ref):
        rows = rows_ref[...].astype(F32)
        rim = rim_ref[...].astype(F32)
        taps = taps_ref[...].astype(F32)
        index = lax.broadcasted_iota(jnp.int32, rows.shape, 0)
        back1 = jnp.where(index == 0, rim[1:2], pltpu.roll(rows, 1, 0))
        back2 = pltpu.roll(rows, 2, 0)
        back2 = jnp.where(index == 0, rim[0:1], jnp.where(index == 1, rim[1:2], back2))
        return taps[0:1] * rows + taps[1:2] * back1 + taps[2:3] * back2

    query_ref[...] = featurized(q_ref, rq_ref, wq_ref)
    gated = featurized(k_ref, rk_ref, wk_ref) * featurized(v_ref, rv_ref, wv_ref)
    gated_ref[...] = gated.astype(BF16)


def side(projected, rim, short_filter):
    tok = projected.shape[0]
    width = projected.shape[1] // 3
    steps = 8
    cols = width // steps

    def thirds(rows):
        return [
            pl.BlockSpec((rows, cols), functools.partial(lambda third, i: (0, i + third * steps), t))
            for t in range(3)
        ]

    wide = pl.BlockSpec((tok, cols), lambda i: (0, i))
    return pl.pallas_call(
        side_kernel,
        grid=(steps,),
        in_specs=thirds(tok)
        + thirds(rim.shape[0])
        + thirds(short_filter.shape[0]),
        out_specs=[wide, wide],
        out_shape=[
            pltpu.HBM((tok, width), F32),
            pltpu.HBM((tok, width), BF16),
        ],
        compiler_params=pltpu.CompilerParams(vmem_limit_bytes=8 << 20),
        name="side",
    )(*[in_hbm(projected)] * 3, *[rim] * 3, *[short_filter] * 3)


def shards(projected, short_filter, long_filter, skip):
    devices = lax.axis_size(AXES)
    tok, width = long_filter.shape
    own = width // devices
    tap_count = short_filter.shape[0]
    rim_count = tap_count - 1
    consts = tables(devices, tok)
    position = lax.axis_index(AXES)
    taps = jnp.concatenate(
        [
            lax.dynamic_slice_in_dim(short_filter, third * width + position * own, own, 1)
            for third in (1, 2)
        ],
        0,
    ).astype(F32)
    taps = jnp.pad(taps, ((0, 8 - 2 * tap_count), (0, tok - own)))
    send = gate(projected, short_filter, long_filter, devices)
    received = lax.all_to_all(send, AXES, split_axis=0, concat_axis=0, tiled=True)
    rim = lax.ppermute(projected[tok - rim_count :], AXES, [(i, i + 1) for i in range(devices - 1)])
    query, gated = side(projected, rim, short_filter)
    conv = spectral(received, taps, consts)
    conv = lax.all_to_all(conv, AXES, split_axis=0, concat_axis=0, tiled=True)
    return mix(conv, query, skip[None, :], gated)


def solution(mesh):
    in_specs = (P(AXES, None), P(), P(AXES, None), P())
    return jax.shard_map(
        shards, mesh=mesh, in_specs=in_specs, out_specs=P(AXES, None), check_vma=False
    )
```

```python
import functools
import math

import jax
import jax.numpy as jnp
import numpy as np
from jax import lax
from jax.experimental import pallas as pl
from jax.experimental.pallas import tpu as pltpu
from jax.sharding import PartitionSpec as P


AXES = ("outer", "inner")
F32 = jnp.float32
BF16 = jnp.bfloat16
PAD = 1


def turn_table(rows, cols, length):
    product = (np.asarray(rows, np.int64) * np.asarray(cols, np.int64)) % length
    angle = product.astype(np.float32) * np.float32(2.0 * math.pi / length)
    angle = angle.astype(np.float64)
    return np.cos(angle).astype(np.float32), np.sin(angle).astype(np.float32)


def paired(reals, imags):
    both = np.stack([reals.reshape(-1, 8, reals.shape[1]), imags.reshape(-1, 8, imags.shape[1])], 1)
    return both.reshape(-1, reals.shape[1])


def tables(segments, tok):
    half = segments
    blocks = 2 * segments
    transform = blocks * tok
    kb = np.arange(half + 1)
    cos_b, sin_b = turn_table(kb[:, None], np.arange(segments)[None, :], blocks)
    first = paired(cos_b[:half], np.concatenate([cos_b[half:], -sin_b[1:half]], 0))
    weight = np.full((half + 1,), 2.0, np.float32)
    weight[0] = weight[half] = 1.0
    cos_w = cos_b.astype(BF16).astype(np.float32) * weight[:, None]
    sin_w = sin_b.astype(BF16).astype(np.float32) * weight[:, None]
    last = np.concatenate([cos_w[:half], cos_w[half:], -sin_w[1:half]], 0).T / transform
    cos_l, sin_l = turn_table(np.arange(tok)[:, None], np.arange(tok)[None, :], tok)
    forward = np.block([[cos_l, -sin_l], [sin_l, cos_l]])
    backward = np.block([[cos_l, sin_l], [-sin_l, cos_l]])
    turn_cos, turn_sin = turn_table(kb[:, None], np.arange(tok)[None, :], transform)
    return (
        first.astype(BF16),
        forward.astype(BF16),
        backward.astype(BF16),
        last.astype(BF16),
        turn_cos[:half],
        turn_sin[:half],
        turn_cos[half:],
        turn_sin[half:],
    )


EXTRA = 8


def in_hbm(value):
    return pltpu.with_memory_space_constraint(value, pltpu.HBM)


def gate_kernel(p_ref, f_ref, t_ref, send_ref, w_ref, k_buf, v_buf, f_buf, out_buf, k_ext, v_ext, e_ext, sem, tap_sem):
    tok, width = f_ref.shape
    devices, _, _ = send_ref.shape
    own = width // devices
    steps = sem.shape[0]
    cols = width // steps
    peers = devices // steps

    def reads(i):
        at = pl.ds(i * cols, cols)
        return (
            pltpu.make_async_copy(
                p_ref.at[:, pl.ds(width + i * cols, cols)], k_buf.at[:, at], sem.at[i, 0]
            ),
            pltpu.make_async_copy(
                p_ref.at[:, pl.ds(2 * width + i * cols, cols)], v_buf.at[:, at], sem.at[i, 1]
            ),
            pltpu.make_async_copy(f_ref.at[:, at], f_buf.at[:, at], sem.at[i, 2]),
        )

    def write(i):
        at = pl.ds(i * peers, peers)
        return pltpu.make_async_copy(out_buf.at[at], send_ref.at[at], sem.at[i, 3])

    taps_read = pltpu.make_async_copy(t_ref, w_ref, tap_sem)
    taps_read.start()
    for i in range(steps):
        for copy in reads(i):
            copy.start()
    lead = 8
    lanes = k_ext.shape[2]
    for j in range(cols // lanes):
        k_ext[j, :lead] = jnp.zeros((lead, lanes), F32)
        v_ext[j, :lead] = jnp.zeros((lead, lanes), F32)
    taps_read.wait()
    for i in range(steps):
        for copy in reads(i):
            copy.wait()
        for j in range(cols // lanes):
            start = i * cols + j * lanes
            at = slice(start, start + lanes)

            def featurized(buf, ext, base):
                taps = w_ref[:, base + start : base + start + lanes].astype(F32)
                ext[j, lead:] = buf[:, at].astype(F32)
                return (
                    taps[0:1] * ext[j, lead : lead + tok]
                    + taps[1:2] * ext[j, pl.ds(lead - 1, tok)]
                    + taps[2:3] * ext[j, pl.ds(lead - 2, tok)]
                )

            gated = featurized(k_buf, k_ext, width) * featurized(v_buf, v_ext, 2 * width)
            near = lanes // own
            to = slice(start // own, start // own + near)
            out_buf[to, :own] = gated.astype(BF16).T.reshape(near, own, tok)
            out_buf[to, own : 2 * own] = f_buf[:, at].T.reshape(near, own, tok)
            e_ext[0:2] = k_ext[j, lead : lead + 2]
            e_ext[2:4] = v_ext[j, lead : lead + 2]
            e_ext[4:6] = k_ext[j, lead + tok - 2 : lead + tok]
            e_ext[6:8] = v_ext[j, lead + tok - 2 : lead + tok]
            tile = e_ext[...]
            for k in range(near):
                turned = pltpu.roll(tile, lanes - k * own, 1) if k else tile
                out_buf[start // own + k, 2 * own :] = turned.astype(BF16)
        write(i).start()
    for i in range(steps):
        write(i).wait()


def gate(projected, short_filter, long_filter, devices):
    tok, width = long_filter.shape
    own = width // devices
    steps = 8
    cols = width // steps
    rows = 2 * own + EXTRA
    return pl.pallas_call(
        gate_kernel,
        in_specs=[
            pl.BlockSpec(memory_space=pltpu.HBM),
            pl.BlockSpec(memory_space=pltpu.HBM),
            pl.BlockSpec(memory_space=pltpu.HBM),
        ],
        out_specs=pl.BlockSpec(memory_space=pltpu.HBM),
        out_shape=pltpu.HBM((devices, rows, tok), BF16),
        scratch_shapes=[
            pltpu.VMEM(short_filter.shape, BF16),
            pltpu.VMEM((tok, width), BF16),
            pltpu.VMEM((tok, width), BF16),
            pltpu.VMEM((tok, width), BF16),
            pltpu.VMEM((devices, rows, tok), BF16),
            pltpu.VMEM((cols // 128, tok + 8, 128), F32),
            pltpu.VMEM((cols // 128, tok + 8, 128), F32),
            pltpu.VMEM((EXTRA, 128), F32),
            pltpu.SemaphoreType.DMA((steps, 4)),
            pltpu.SemaphoreType.DMA(()),
        ],
        compiler_params=pltpu.CompilerParams(vmem_limit_bytes=16 << 20),
        name="gate",
    )(in_hbm(projected), in_hbm(long_filter), in_hbm(short_filter))


def dot(a, b):
    return jnp.dot(a, b, preferred_element_type=F32)


def spectral_kernel(
    z_ref, taps_ref, first_ref, fwd_ref, bwd_ref, last_ref, tc_ref, ts_ref, hc_ref, hs_ref,
    out_ref, rows_ref, fix_ref, spec_ref, half_ref, half_out_ref, prod_ref, back_ref, conv_ref, block_ref, sem,
):
    segments, rows, tok = z_ref.shape
    both = rows - EXTRA
    own = both // 2
    pitch = rows_ref.shape[0] // (segments + 1)
    out_pitch = conv_ref.shape[0] // segments
    piece = 16

    def widen(i, carry):
        for j in range(piece):
            b = i * piece + j
            rows_ref[pl.ds((b + 1) * pitch, rows), :] = z_ref[b].astype(F32)
        return carry

    lax.fori_loop(0, segments // piece, widen, 0)

    rows_ref[both:rows, :] = jnp.zeros((EXTRA, tok), F32)

    def sent(row, before):
        return rows_ref[pl.ds(both + row + (1 - before) * pitch, segments, stride=pitch), :]

    def edge(tap, at):
        now0, now1 = sent(at, 0), sent(at + 1, 0)
        ago2, ago1 = sent(at + 4, 1), sent(at + 5, 1)
        taps = [taps_ref[tap + n : tap + n + 1, :] for n in range(3)]
        return (
            taps[0] * now0 + taps[1] * ago1 + taps[2] * ago2,
            taps[0] * now1 + taps[1] * now0 + taps[2] * ago1,
        )

    key0, key1 = edge(0, 0)
    value0, value1 = edge(3, 2)
    gated0 = key0 * value0
    gated1 = pltpu.roll(key1 * value1, 1, 1)
    lane = lax.broadcasted_iota(jnp.int32, (segments, tok), 1)
    fix_ref[0] = jnp.where(lane % 2 == 0, gated0, gated1)
    fix_ref[1] = jnp.where(lane % 2 == 1, gated0, gated1)

    top = 8
    index = lax.broadcasted_iota(jnp.int32, (top, tok), 0)

    def first_row(row, block):
        return jnp.concatenate([jnp.where(index == 0, row, block[:top]), block[top:]], 0)

    group, group2, group3, group4 = 16, 16, 16, 32

    run = 16

    def first_section(which, i, carry):
        start = i * group
        base = which * own + start
        cols = []
        for j in range(group):
            col = rows_ref[pl.ds(base + j + pitch, segments, stride=pitch), :]
            if which == 0:
                fixed = pltpu.roll(fix_ref[j % 2], (tok - start - j) % tok, 1)
                col = jnp.where(lane < 2, fixed, col)
            cols.append(col.astype(BF16))
        out = dot(first_ref[...], jnp.concatenate(cols, 1))
        out = out.reshape(segments // top, 2, top, group * tok)
        tc, ts = tc_ref[...], ts_ref[...]
        for j in range(group):
            real = out[:, 0, :, j * tok : (j + 1) * tok].reshape(segments, tok)
            imag = out[:, 1, :, j * tok : (j + 1) * tok].reshape(segments, tok)
            half_ref[pl.ds(base + j, 1), :] = imag[0:1]
            imag = first_row(0.0, imag)
            both_parts = jnp.concatenate([real * tc + imag * ts, imag * tc - real * ts], 1)
            both_parts = both_parts.astype(BF16).reshape(segments // run, run, 2 * tok)
            spec_ref[start + j, :, which] = both_parts
        return carry

    for which in range(2):
        lax.fori_loop(0, own // group, functools.partial(first_section, which), 0)

    def product(sig, fil):
        sr, si, fr, fi = sig[:, :tok], sig[:, tok:], fil[:, :tok], fil[:, tok:]
        return jnp.concatenate(
            [(sr * fr - si * fi).astype(BF16), (sr * fi + si * fr).astype(BF16)], 1
        )

    half = half_ref[...]
    hc, hs = hc_ref[...], hs_ref[...]
    half = jnp.concatenate([(half * hc).astype(BF16), (-half * hs).astype(BF16)], 1)
    half = dot(half, fwd_ref[...])
    half = dot(product(half[:own], half[own:]), bwd_ref[...])
    half_out_ref[...] = half[:, :tok] * hc - half[:, tok:] * hs

    def multiply(i, carry):
        start = i * group2
        spec = spec_ref[pl.ds(start, group2)].reshape(group2 * 2 * segments, 2 * tok)
        spec = dot(spec, fwd_ref[...]).reshape(group2 * segments // run, 2, run, 2 * tok)
        sig = spec[:, 0].reshape(group2 * segments, 2 * tok)
        fil = spec[:, 1].reshape(group2 * segments, 2 * tok)
        prod_ref[pl.ds(start, group2)] = product(sig, fil).reshape(group2, segments, 2 * tok)
        return carry

    lax.fori_loop(0, own // group2, multiply, 0)

    def invert(i, carry):
        start = i * group3
        tc, ts = tc_ref[...], ts_ref[...]
        back = dot(
            prod_ref[pl.ds(start, group3)].reshape(group3 * segments, 2 * tok), bwd_ref[...]
        )
        for j in range(group3):
            br = back[j * segments : (j + 1) * segments, :tok]
            bi = back[j * segments : (j + 1) * segments, tok:]
            imag = first_row(half_out_ref[pl.ds(start + j, 1), :], bi * tc + br * ts)
            back_ref[start + j, :segments] = (br * tc - bi * ts).astype(BF16)
            back_ref[start + j, segments:] = imag.astype(BF16)
        return carry

    lax.fori_loop(0, own // group3, invert, 0)

    def finish(i, carry):
        start = i * group4
        stacked = jnp.concatenate([back_ref[start + j] for j in range(group4)], 1)
        conv = dot(last_ref[...], stacked)
        for j in range(group4):
            conv_ref[pl.ds(start + j, segments, stride=out_pitch), :] = conv[
                :, j * tok : (j + 1) * tok
            ]
        return carry

    lax.fori_loop(0, own // group4, finish, 0)

    def write(i):
        at = pl.ds(i * piece, piece)
        return pltpu.make_async_copy(block_ref.at[at], out_ref.at[at], sem.at[i])

    for i in range(segments // piece):
        for b in range(i * piece, (i + 1) * piece):
            block_ref[b] = conv_ref[b * out_pitch : b * out_pitch + own, :].astype(BF16)
        write(i).start()
    for i in range(segments // piece):
        write(i).wait()


def spectral(received, taps, consts):
    segments, rows, tok = received.shape
    both = rows - EXTRA
    own = both // 2
    return pl.pallas_call(
        spectral_kernel,
        out_shape=pltpu.HBM((segments, own, tok), BF16),
        in_specs=[pl.BlockSpec(memory_space=pltpu.VMEM)] * 10,
        out_specs=pl.BlockSpec(memory_space=pltpu.HBM),
        scratch_shapes=[
            pltpu.VMEM(((segments + 1) * (rows + PAD), tok), F32),
            pltpu.VMEM((2, segments, tok), F32),
            pltpu.VMEM((own, segments // 16, 2, 16, 2 * tok), BF16),
            pltpu.VMEM((both, tok), F32),
            pltpu.VMEM((own, tok), F32),
            pltpu.VMEM((own, segments, 2 * tok), BF16),
            pltpu.VMEM((own, 2 * segments, tok), BF16),
            pltpu.VMEM((segments * (own + PAD), tok), F32),
            pltpu.VMEM((segments, own, tok), BF16),
            pltpu.SemaphoreType.DMA((segments // 16,)),
        ],
        compiler_params=pltpu.CompilerParams(vmem_limit_bytes=28 << 20),
        name="spectral",
    )(resident(received), taps, *consts)


def mix_kernel(c_ref, q_ref, skip_ref, g_ref, out_ref, buf_ref, sem):
    peers, own, tok = c_ref.shape
    steps = sem.shape[0]
    peers = peers // steps
    cols = peers * own
    near = 128 // own

    def write(i):
        at = pl.ds(i * cols, cols)
        return pltpu.make_async_copy(buf_ref.at[:, at], out_ref.at[:, at], sem.at[i])

    for i in range(steps):
        for j in range(i * peers, (i + 1) * peers, near):
            at = slice(j * own, (j + near) * own)
            conv = c_ref[j : j + near].reshape(near * own, tok).T.astype(F32)
            direct = skip_ref[:, at] * g_ref[:, at].astype(F32)
            buf_ref[:, at] = (q_ref[:, at].astype(F32) * (conv + direct)).astype(BF16)
        write(i).start()
    for i in range(steps):
        write(i).wait()


def resident(value):
    return pltpu.with_memory_space_constraint(value, pltpu.VMEM)


def mix(conv, query, skip, gated):
    devices, own, tok = conv.shape
    width = devices * own
    steps = 8
    return pl.pallas_call(
        mix_kernel,
        in_specs=[pl.BlockSpec(memory_space=pltpu.VMEM)] * 4,
        out_specs=pl.BlockSpec(memory_space=pltpu.HBM),
        out_shape=jax.ShapeDtypeStruct((tok, width), BF16),
        scratch_shapes=[
            pltpu.VMEM((tok, width), BF16),
            pltpu.SemaphoreType.DMA((steps,)),
        ],
        compiler_params=pltpu.CompilerParams(vmem_limit_bytes=6 << 20),
        name="mix",
    )(resident(conv), resident(query), resident(skip), resident(gated))


def side_kernel(q_ref, k_ref, v_ref, rq_ref, rk_ref, rv_ref, wq_ref, wk_ref, wv_ref,
                query_ref, gated_ref):
    def featurized(rows_ref, rim_ref, taps_ref):
        rows = rows_ref[...].astype(F32)
        rim = rim_ref[...].astype(F32)
        taps = taps_ref[...].astype(F32)
        index = lax.broadcasted_iota(jnp.int32, rows.shape, 0)
        back1 = jnp.where(index == 0, rim[1:2], pltpu.roll(rows, 1, 0))
        back2 = pltpu.roll(rows, 2, 0)
        back2 = jnp.where(index == 0, rim[0:1], jnp.where(index == 1, rim[1:2], back2))
        return taps[0:1] * rows + taps[1:2] * back1 + taps[2:3] * back2

    query_ref[...] = featurized(q_ref, rq_ref, wq_ref).astype(BF16)
    gated = featurized(k_ref, rk_ref, wk_ref) * featurized(v_ref, rv_ref, wv_ref)
    gated_ref[...] = gated.astype(BF16)


def side(projected, rim, short_filter):
    tok = projected.shape[0]
    width = projected.shape[1] // 3
    steps = 8
    cols = width // steps

    def thirds(rows):
        return [
            pl.BlockSpec((rows, cols), functools.partial(lambda third, i: (0, i + third * steps), t))
            for t in range(3)
        ]

    wide = pl.BlockSpec((tok, cols), lambda i: (0, i))
    return pl.pallas_call(
        side_kernel,
        grid=(steps,),
        in_specs=thirds(tok)
        + thirds(rim.shape[0])
        + thirds(short_filter.shape[0]),
        out_specs=[wide, wide],
        out_shape=[
            jax.ShapeDtypeStruct((tok, width), BF16),
            jax.ShapeDtypeStruct((tok, width), BF16),
        ],
        compiler_params=pltpu.CompilerParams(vmem_limit_bytes=8 << 20),
        name="side",
    )(*[in_hbm(projected)] * 3, *[rim] * 3, *[short_filter] * 3)


def shards(projected, short_filter, long_filter, skip):
    devices = lax.axis_size(AXES)
    tok, width = long_filter.shape
    own = width // devices
    tap_count = short_filter.shape[0]
    rim_count = tap_count - 1
    consts = tables(devices, tok)
    position = lax.axis_index(AXES)
    taps = jnp.concatenate(
        [
            lax.dynamic_slice_in_dim(short_filter, third * width + position * own, own, 1)
            for third in (1, 2)
        ],
        0,
    ).astype(F32)
    taps = jnp.pad(taps, ((0, 8 - 2 * tap_count), (0, tok - own)))
    send = gate(projected, short_filter, long_filter, devices)
    received = lax.all_to_all(send, AXES, split_axis=0, concat_axis=0, tiled=True)
    rim = lax.ppermute(projected[tok - rim_count :], AXES, [(i, i + 1) for i in range(devices - 1)])
    query, gated = side(projected, rim, short_filter)
    conv = spectral(received, taps, consts)
    conv = lax.all_to_all(conv, AXES, split_axis=0, concat_axis=0, tiled=True)
    return mix(conv, query, skip[None, :], gated)


def solution(mesh):
    in_specs = (P(AXES, None), P(), P(AXES, None), P())
    return jax.shard_map(
        shards, mesh=mesh, in_specs=in_specs, out_specs=P(AXES, None), check_vma=False
    )
```

```python
import functools
import math

import jax
import jax.numpy as jnp
import numpy as np
from jax import lax
from jax.experimental import pallas as pl
from jax.experimental.pallas import tpu as pltpu
from jax.sharding import PartitionSpec as P


AXES = ("outer", "inner")
TURNED = ("inner", "outer")
F32 = jnp.float32
BF16 = jnp.bfloat16
PAD = 1


def turn_table(rows, cols, length):
    product = (np.asarray(rows, np.int64) * np.asarray(cols, np.int64)) % length
    angle = product.astype(np.float32) * np.float32(2.0 * math.pi / length)
    angle = angle.astype(np.float64)
    return np.cos(angle).astype(np.float32), np.sin(angle).astype(np.float32)


def paired(reals, imags):
    both = np.stack([reals.reshape(-1, 8, reals.shape[1]), imags.reshape(-1, 8, imags.shape[1])], 1)
    return both.reshape(-1, reals.shape[1])


def tables(order, tok):
    segments = len(order)
    half = segments
    blocks = 2 * segments
    transform = blocks * tok
    kb = np.arange(half + 1)
    cos_b, sin_b = turn_table(kb[:, None], np.asarray(order)[None, :], blocks)
    first = paired(cos_b[:half], np.concatenate([cos_b[half:], -sin_b[1:half]], 0))
    weight = np.full((half + 1,), 2.0, np.float32)
    weight[0] = weight[half] = 1.0
    cos_w = cos_b.astype(BF16).astype(np.float32) * weight[:, None]
    sin_w = sin_b.astype(BF16).astype(np.float32) * weight[:, None]
    last = np.concatenate([cos_w[:half], cos_w[half:], -sin_w[1:half]], 0).T / transform
    cos_l, sin_l = turn_table(np.arange(tok)[:, None], np.arange(tok)[None, :], tok)
    forward = np.block([[cos_l, -sin_l], [sin_l, cos_l]])
    backward = np.block([[cos_l, sin_l], [-sin_l, cos_l]])
    turn_cos, turn_sin = turn_table(kb[:, None], np.arange(tok)[None, :], transform)
    return (
        first.astype(BF16),
        forward.astype(BF16),
        backward.astype(BF16),
        last.astype(BF16),
        turn_cos[:half],
        turn_sin[:half],
        turn_cos[half:],
        turn_sin[half:],
    )


EXTRA = 2


def in_hbm(value):
    return pltpu.with_memory_space_constraint(value, pltpu.HBM)


def gate_kernel(
    own, p_ref, f_ref, t_ref, send_ref, w_ref, k_buf, v_buf, f_buf, out_buf, k_ext, v_ext, e_ext,
    stage, sem, tap_sem,
):
    tok, width = f_ref.shape
    run = 2 * own + EXTRA
    steps = sem.shape[0]
    cols = width // steps
    lanes = e_ext.shape[2]
    near = lanes // own
    chunk = cols // own * run
    ahead = 2

    def reads(i):
        at = pl.ds(i * cols, cols)
        return (
            pltpu.make_async_copy(
                p_ref.at[:, pl.ds(width + i * cols, cols)], k_buf.at[:, at], sem.at[i, 0]
            ),
            pltpu.make_async_copy(
                p_ref.at[:, pl.ds(2 * width + i * cols, cols)], v_buf.at[:, at], sem.at[i, 1]
            ),
            pltpu.make_async_copy(f_ref.at[:, at], f_buf.at[:, at], sem.at[i, 2]),
        )

    def write(i):
        at = pl.ds(i * chunk, chunk)
        return pltpu.make_async_copy(out_buf.at[at], send_ref.at[at], sem.at[i, 3])

    taps_read = pltpu.make_async_copy(t_ref, w_ref, tap_sem)
    taps_read.start()
    for i in range(ahead):
        for copy in reads(i):
            copy.start()
    lead = 8
    for j in range(cols // lanes):
        k_ext[j, :lead] = jnp.zeros((lead, lanes), F32)
        v_ext[j, :lead] = jnp.zeros((lead, lanes), F32)
    row = lax.broadcasted_iota(jnp.int32, (8, lanes), 0) % 4
    piece = lax.broadcasted_iota(jnp.int32, (8, lanes), 1) // own
    taps_read.wait()
    for i in range(steps):
        for copy in reads(i):
            copy.wait()
        if i + ahead < steps:
            for copy in reads(i + ahead):
                copy.start()
        for j in range(cols // lanes):
            start = i * cols + j * lanes
            at = slice(start, start + lanes)

            def featurized(buf, ext, base):
                taps = w_ref[:, base + start : base + start + lanes].astype(F32)
                ext[j, lead:] = buf[:, at].astype(F32)
                return (
                    taps[0:1] * ext[j, lead : lead + tok]
                    + taps[1:2] * ext[j, pl.ds(lead - 1, tok)]
                    + taps[2:3] * ext[j, pl.ds(lead - 2, tok)]
                )

            gated = featurized(k_buf, k_ext, width) * featurized(v_buf, v_ext, 2 * width)
            gated = gated.astype(BF16).T.astype(F32)
            taken = f_buf[:, at].T.astype(F32)
            e_ext[j, 0:2] = k_ext[j, lead : lead + 2]
            e_ext[j, 2:4] = v_ext[j, lead : lead + 2]
            e_ext[j, 4:6] = k_ext[j, lead + tok - 2 : lead + tok]
            e_ext[j, 6:8] = v_ext[j, lead + tok - 2 : lead + tok]
            edge = e_ext[j]
            turned = edge
            for m in range(1, near):
                turned = jnp.where(row == m, pltpu.roll(edge, m * own, 1), turned)
            for k in range(near):
                to = (j * near + k) * run
                mine = slice(k * own, (k + 1) * own)
                stage[i % 2, to : to + own, :] = gated[mine]
                stage[i % 2, to + own : to + 2 * own, :] = taken[mine]
                part = pltpu.roll(turned, lanes - k * own, 1) if k else turned
                part = jnp.where(row == piece, part, 0.0)
                part = part + pltpu.roll(part, 7, 0)
                part = part + pltpu.roll(part, 6, 0)
                stage[i % 2, to + 2 * own : to + 2 * own + 1, :] = part[0:1]
                stage[i % 2, to + 2 * own + 1 : to + 2 * own + 2, :] = part[4:5]
        out_buf[i * chunk : (i + 1) * chunk] = stage[i % 2].astype(BF16)
        write(i).start()
    for i in range(steps):
        write(i).wait()


def gate(projected, short_filter, long_filter, devices):
    tok, width = long_filter.shape
    own = width // devices
    steps = 8
    cols = width // steps
    run = 2 * own + EXTRA
    return pl.pallas_call(
        functools.partial(gate_kernel, own),
        in_specs=[pl.BlockSpec(memory_space=pltpu.HBM)] * 3,
        out_specs=pl.BlockSpec(memory_space=pltpu.HBM),
        out_shape=pltpu.HBM((devices * run, tok), BF16),
        scratch_shapes=[
            pltpu.VMEM(short_filter.shape, BF16),
            pltpu.VMEM((tok, width), BF16),
            pltpu.VMEM((tok, width), BF16),
            pltpu.VMEM((tok, width), BF16),
            pltpu.VMEM((devices * run, tok), BF16),
            pltpu.VMEM((cols // 128, tok + 8, 128), F32),
            pltpu.VMEM((cols // 128, tok + 8, 128), F32),
            pltpu.VMEM((cols // 128, 8, 128), F32),
            pltpu.VMEM((2, cols // own * run, 128), F32),
            pltpu.SemaphoreType.DMA((steps, 4)),
            pltpu.SemaphoreType.DMA(()),
        ],
        compiler_params=pltpu.CompilerParams(vmem_limit_bytes=20 << 20),
        name="gate",
    )(in_hbm(projected), in_hbm(long_filter), in_hbm(short_filter))


def dot(a, b):
    return jnp.dot(a, b, preferred_element_type=F32)


def spectral_kernel(
    outer, z_ref, taps_ref, first_ref, fwd_ref, bwd_ref, last_ref, tc_ref, ts_ref, hc_ref, hs_ref,
    out_ref, rows_ref, fix_ref, spec_ref, half_ref, half_out_ref, prod_ref, back_ref, conv_ref, block_ref, sem,
):
    segments, own, tok = out_ref.shape
    both = 2 * own
    pitch = both + EXTRA
    out_pitch = conv_ref.shape[0] // segments
    piece = 16
    rim = outer * pitch

    def widen(i, carry):
        start = pl.multiple_of(i * (piece * pitch), piece * pitch)
        block = z_ref[pl.ds(start, piece * pitch), :].astype(F32)
        rows_ref[pl.ds(rim + start, piece * pitch), :] = block
        return carry

    lax.fori_loop(0, segments // piece, widen, 0)

    rows_ref[pitch - 1 : pitch, :] = jnp.zeros((1, tok), F32)
    for o in range(1, outer):
        last = (segments + o - 1) * pitch + pitch - 1
        rows_ref[o * pitch + pitch - 1 : (o + 1) * pitch, :] = rows_ref[last : last + 1, :]
    now = rows_ref[pl.ds(rim + both, segments, stride=pitch), :]
    ago = rows_ref[pl.ds(both + 1, segments, stride=pitch), :]
    lane = lax.broadcasted_iota(jnp.int32, (segments, tok), 1)
    middle = jnp.where(
        lane // own % 2 == 0, pltpu.roll(ago, tok - own, 1), pltpu.roll(now, own, 1)
    )
    edges = taps_ref[0:1, :] * now + taps_ref[1:2, :] * middle + taps_ref[2:3, :] * ago
    edges = edges * pltpu.roll(edges, tok - 2 * own, 1)
    after = pltpu.roll(edges, tok - own + 1, 1)
    fix_ref[0] = jnp.where(lane % 2 == 0, edges, after)
    fix_ref[1] = jnp.where(lane % 2 == 1, edges, after)

    top = 8
    index = lax.broadcasted_iota(jnp.int32, (top, tok), 0)

    def first_row(row, block):
        return jnp.concatenate([jnp.where(index == 0, row, block[:top]), block[top:]], 0)

    group, group2, group3, group4 = 16, 16, 16, 32

    run = 16

    def first_section(which, i, carry):
        start = i * group
        base = which * own + start
        cols = []
        for j in range(group):
            col = rows_ref[pl.ds(rim + base + j, segments, stride=pitch), :]
            if which == 0:
                fixed = pltpu.roll(fix_ref[j % 2], (tok - start - j) % tok, 1)
                col = jnp.where(lane < 2, fixed, col)
            cols.append(col.astype(BF16))
        out = dot(first_ref[...], jnp.concatenate(cols, 1))
        out = out.reshape(segments // top, 2, top, group * tok)
        tc, ts = tc_ref[...], ts_ref[...]
        for j in range(group):
            real = out[:, 0, :, j * tok : (j + 1) * tok].reshape(segments, tok)
            imag = out[:, 1, :, j * tok : (j + 1) * tok].reshape(segments, tok)
            half_ref[pl.ds(base + j, 1), :] = imag[0:1]
            imag = first_row(0.0, imag)
            both_parts = jnp.concatenate([real * tc + imag * ts, imag * tc - real * ts], 1)
            both_parts = both_parts.astype(BF16).reshape(segments // run, run, 2 * tok)
            spec_ref[start + j, :, which] = both_parts
        return carry

    for which in range(2):
        lax.fori_loop(0, own // group, functools.partial(first_section, which), 0)

    def product(sig, fil):
        sr, si, fr, fi = sig[:, :tok], sig[:, tok:], fil[:, :tok], fil[:, tok:]
        return jnp.concatenate(
            [(sr * fr - si * fi).astype(BF16), (sr * fi + si * fr).astype(BF16)], 1
        )

    half = half_ref[...]
    hc, hs = hc_ref[...], hs_ref[...]
    half = jnp.concatenate([(half * hc).astype(BF16), (-half * hs).astype(BF16)], 1)
    half = dot(half, fwd_ref[...])
    half = dot(product(half[:own], half[own:]), bwd_ref[...])
    half_out_ref[...] = half[:, :tok] * hc - half[:, tok:] * hs

    def multiply(i, carry):
        start = i * group2
        spec = spec_ref[pl.ds(start, group2)].reshape(group2 * 2 * segments, 2 * tok)
        spec = dot(spec, fwd_ref[...]).reshape(group2 * segments // run, 2, run, 2 * tok)
        sig = spec[:, 0].reshape(group2 * segments, 2 * tok)
        fil = spec[:, 1].reshape(group2 * segments, 2 * tok)
        prod_ref[pl.ds(start, group2)] = product(sig, fil).reshape(group2, segments, 2 * tok)
        return carry

    lax.fori_loop(0, own // group2, multiply, 0)

    def invert(i, carry):
        start = i * group3
        tc, ts = tc_ref[...], ts_ref[...]
        back = dot(
            prod_ref[pl.ds(start, group3)].reshape(group3 * segments, 2 * tok), bwd_ref[...]
        )
        for j in range(group3):
            br = back[j * segments : (j + 1) * segments, :tok]
            bi = back[j * segments : (j + 1) * segments, tok:]
            imag = first_row(half_out_ref[pl.ds(start + j, 1), :], bi * tc + br * ts)
            back_ref[start + j, :segments] = (br * tc - bi * ts).astype(BF16)
            back_ref[start + j, segments:] = imag.astype(BF16)
        return carry

    lax.fori_loop(0, own // group3, invert, 0)

    def finish(i, carry):
        start = i * group4
        stacked = jnp.concatenate([back_ref[start + j] for j in range(group4)], 1)
        conv = dot(last_ref[...], stacked)
        for j in range(group4):
            conv_ref[pl.ds(start + j, segments, stride=out_pitch), :] = conv[
                :, j * tok : (j + 1) * tok
            ]
        return carry

    lax.fori_loop(0, own // group4, finish, 0)

    def write(i):
        at = pl.ds(i * piece, piece)
        return pltpu.make_async_copy(block_ref.at[at], out_ref.at[at], sem.at[i])

    for i in range(segments // piece):
        for b in range(i * piece, (i + 1) * piece):
            block_ref[b] = conv_ref[b * out_pitch : b * out_pitch + own, :].astype(BF16)
        write(i).start()
    for i in range(segments // piece):
        write(i).wait()


def spectral(received, taps, consts, outer, own):
    tok = received.shape[1]
    both = 2 * own
    pitch = both + EXTRA
    segments = received.shape[0] // pitch
    return pl.pallas_call(
        functools.partial(spectral_kernel, outer),
        out_shape=pltpu.HBM((segments, own, tok), BF16),
        in_specs=[pl.BlockSpec(memory_space=pltpu.VMEM)] * 10,
        out_specs=pl.BlockSpec(memory_space=pltpu.HBM),
        scratch_shapes=[
            pltpu.VMEM(((segments + outer) * pitch, tok), F32),
            pltpu.VMEM((2, segments, tok), F32),
            pltpu.VMEM((own, segments // 16, 2, 16, 2 * tok), BF16),
            pltpu.VMEM((both, tok), F32),
            pltpu.VMEM((own, tok), F32),
            pltpu.VMEM((own, segments, 2 * tok), BF16),
            pltpu.VMEM((own, 2 * segments, tok), BF16),
            pltpu.VMEM((segments * (own + PAD), tok), F32),
            pltpu.VMEM((segments, own, tok), BF16),
            pltpu.SemaphoreType.DMA((segments // 16,)),
        ],
        compiler_params=pltpu.CompilerParams(vmem_limit_bytes=28 << 20),
        name="spectral",
    )(resident(received), taps, *consts)


def mix_kernel(c_ref, q_ref, skip_ref, g_ref, out_ref, buf_ref, sem):
    peers, own, tok = c_ref.shape
    steps = sem.shape[0]
    peers = peers // steps
    cols = peers * own
    near = 128 // own

    def write(i):
        at = pl.ds(i * cols, cols)
        return pltpu.make_async_copy(buf_ref.at[:, at], out_ref.at[:, at], sem.at[i])

    for i in range(steps):
        for j in range(i * peers, (i + 1) * peers, near):
            at = slice(j * own, (j + near) * own)
            conv = c_ref[j : j + near].reshape(near * own, tok).T.astype(F32)
            direct = skip_ref[:, at] * g_ref[:, at].astype(F32)
            buf_ref[:, at] = (q_ref[:, at].astype(F32) * (conv + direct)).astype(BF16)
        write(i).start()
    for i in range(steps):
        write(i).wait()


def resident(value):
    return pltpu.with_memory_space_constraint(value, pltpu.VMEM)


def mix(conv, query, skip, gated):
    devices, own, tok = conv.shape
    width = devices * own
    steps = 8
    return pl.pallas_call(
        mix_kernel,
        in_specs=[pl.BlockSpec(memory_space=pltpu.VMEM)] * 4,
        out_specs=pl.BlockSpec(memory_space=pltpu.HBM),
        out_shape=jax.ShapeDtypeStruct((tok, width), BF16),
        scratch_shapes=[
            pltpu.VMEM((tok, width), BF16),
            pltpu.SemaphoreType.DMA((steps,)),
        ],
        compiler_params=pltpu.CompilerParams(vmem_limit_bytes=6 << 20),
        name="mix",
    )(resident(conv), resident(query), resident(skip), resident(gated))


def side_kernel(q_ref, k_ref, v_ref, rq_ref, rk_ref, rv_ref, wq_ref, wk_ref, wv_ref,
                query_ref, gated_ref):
    def featurized(rows_ref, rim_ref, taps_ref):
        rows = rows_ref[...].astype(F32)
        rim = rim_ref[...].astype(F32)
        taps = taps_ref[...].astype(F32)
        index = lax.broadcasted_iota(jnp.int32, rows.shape, 0)
        back1 = jnp.where(index == 0, rim[1:2], pltpu.roll(rows, 1, 0))
        back2 = pltpu.roll(rows, 2, 0)
        back2 = jnp.where(index == 0, rim[0:1], jnp.where(index == 1, rim[1:2], back2))
        return taps[0:1] * rows + taps[1:2] * back1 + taps[2:3] * back2

    query_ref[...] = featurized(q_ref, rq_ref, wq_ref).astype(BF16)
    gated = featurized(k_ref, rk_ref, wk_ref) * featurized(v_ref, rv_ref, wv_ref)
    gated_ref[...] = gated.astype(BF16)


def side(projected, rim, short_filter):
    tok = projected.shape[0]
    width = projected.shape[1] // 3
    steps = 8
    cols = width // steps

    def thirds(rows):
        return [
            pl.BlockSpec((rows, cols), functools.partial(lambda third, i: (0, i + third * steps), t))
            for t in range(3)
        ]

    wide = pl.BlockSpec((tok, cols), lambda i: (0, i))
    return pl.pallas_call(
        side_kernel,
        grid=(steps,),
        in_specs=thirds(tok)
        + thirds(rim.shape[0])
        + thirds(short_filter.shape[0]),
        out_specs=[wide, wide],
        out_shape=[
            jax.ShapeDtypeStruct((tok, width), BF16),
            jax.ShapeDtypeStruct((tok, width), BF16),
        ],
        compiler_params=pltpu.CompilerParams(vmem_limit_bytes=8 << 20),
        name="side",
    )(*[in_hbm(projected)] * 3, *[rim] * 3, *[short_filter] * 3)


def shards(projected, short_filter, long_filter, skip):
    devices = lax.axis_size(AXES)
    tok, width = long_filter.shape
    own = width // devices
    tap_count = short_filter.shape[0]
    rim_count = tap_count - 1
    outer = lax.axis_size("outer")
    order = np.arange(devices).reshape(outer, -1).T.reshape(-1)
    consts = tables(order, tok)
    position = lax.axis_index(TURNED)
    taps = [
        lax.dynamic_slice_in_dim(short_filter, third * width + position * own, own, 1)
        for third in (1, 2)
    ]
    taps = jnp.concatenate([taps[0], taps[0], taps[1], taps[1]], 1).astype(F32)
    send = gate(projected, short_filter, long_filter, devices)
    pairs = send.reshape(devices, -1, 2, tok)
    received = lax.all_to_all(pairs, TURNED, split_axis=0, concat_axis=0, tiled=True)
    received = received.reshape(send.shape)
    rim = lax.ppermute(projected[tok - rim_count :], AXES, [(i, i + 1) for i in range(devices - 1)])
    query, gated = side(projected, rim, short_filter)
    conv = spectral(received, taps, consts, outer, own)
    conv = lax.all_to_all(conv, TURNED, split_axis=0, concat_axis=0, tiled=True)
    return mix(conv, query, skip[None, :], gated)


def solution(mesh):
    in_specs = (P(AXES, None), P(), P(AXES, None), P())
    return jax.shard_map(
        shards, mesh=mesh, in_specs=in_specs, out_specs=P(AXES, None), check_vma=False
    )
```

```python
import functools
import math

import jax
import jax.numpy as jnp
import numpy as np
from jax import lax
from jax.experimental import pallas as pl
from jax.experimental.pallas import tpu as pltpu
from jax.sharding import PartitionSpec as P


AXES = ("outer", "inner")
TURNED = ("inner", "outer")
F32 = jnp.float32
BF16 = jnp.bfloat16
PAD = 1


def turn_table(rows, cols, length):
    product = (np.asarray(rows, np.int64) * np.asarray(cols, np.int64)) % length
    angle = product.astype(np.float32) * np.float32(2.0 * math.pi / length)
    angle = angle.astype(np.float64)
    return np.cos(angle).astype(np.float32), np.sin(angle).astype(np.float32)


def paired(reals, imags):
    both = np.stack([reals.reshape(-1, 8, reals.shape[1]), imags.reshape(-1, 8, imags.shape[1])], 1)
    return both.reshape(-1, reals.shape[1])


def tables(order, tok):
    segments = len(order)
    half = segments
    blocks = 2 * segments
    transform = blocks * tok
    kb = np.arange(half + 1)
    cos_b, sin_b = turn_table(kb[:, None], np.asarray(order)[None, :], blocks)
    first = paired(cos_b[:half], np.concatenate([cos_b[half:], -sin_b[1:half]], 0))
    weight = np.full((half + 1,), 2.0, np.float32)
    weight[0] = weight[half] = 1.0
    cos_w = cos_b.astype(BF16).astype(np.float32) * weight[:, None]
    sin_w = sin_b.astype(BF16).astype(np.float32) * weight[:, None]
    last = np.concatenate([cos_w[:half], cos_w[half:], -sin_w[1:half]], 0).T / transform
    cos_l, sin_l = turn_table(np.arange(tok)[:, None], np.arange(tok)[None, :], tok)
    forward = np.block([[cos_l, -sin_l], [sin_l, cos_l]])
    backward = np.block([[cos_l, sin_l], [-sin_l, cos_l]])
    turn_cos, turn_sin = turn_table(kb[:, None], np.arange(tok)[None, :], transform)
    return (
        first.astype(BF16),
        forward.astype(BF16),
        backward.astype(BF16),
        last.astype(BF16),
        turn_cos[:half],
        turn_sin[:half],
        turn_cos[half:],
        turn_sin[half:],
    )


EXTRA = 2


def in_hbm(value):
    return pltpu.with_memory_space_constraint(value, pltpu.HBM)


def gate_kernel(
    own, p_ref, f_ref, t_ref, send_ref, w_ref, k_buf, v_buf, f_buf, out_buf, k_ext, v_ext, e_ext,
    stage, sem, tap_sem,
):
    tok, width = f_ref.shape
    run = 2 * own + EXTRA
    steps = sem.shape[0]
    cols = width // steps
    lanes = e_ext.shape[2]
    near = lanes // own
    chunk = cols // own * run
    ahead = 2

    def reads(i):
        start = pl.multiple_of(i * cols, cols)
        at = pl.ds(start, cols)
        return (
            pltpu.make_async_copy(
                p_ref.at[:, pl.ds(width + start, cols)], k_buf.at[:, at], sem.at[i, 0]
            ),
            pltpu.make_async_copy(
                p_ref.at[:, pl.ds(2 * width + start, cols)], v_buf.at[:, at], sem.at[i, 1]
            ),
            pltpu.make_async_copy(f_ref.at[:, at], f_buf.at[:, at], sem.at[i, 2]),
        )

    def write(i):
        at = pl.ds(pl.multiple_of(i * chunk, chunk), chunk)
        return pltpu.make_async_copy(out_buf.at[at], send_ref.at[at], sem.at[i, 3])

    taps_read = pltpu.make_async_copy(t_ref, w_ref, tap_sem)
    taps_read.start()
    for i in range(ahead):
        for copy in reads(i):
            copy.start()
    lead = 8
    for j in range(cols // lanes):
        k_ext[j, :lead] = jnp.zeros((lead, lanes), F32)
        v_ext[j, :lead] = jnp.zeros((lead, lanes), F32)
    row = lax.broadcasted_iota(jnp.int32, (8, lanes), 0) % 4
    piece = lax.broadcasted_iota(jnp.int32, (8, lanes), 1) // own
    taps_read.wait()

    def turn(i, carry):
        for copy in reads(i):
            copy.wait()

        @pl.when(i + ahead < steps)
        def _():
            for copy in reads(i + ahead):
                copy.start()

        for j in range(cols // lanes):
            start = pl.multiple_of(i * cols + j * lanes, lanes)
            at = pl.ds(start, lanes)

            def featurized(buf, ext, base):
                taps = w_ref[:, pl.ds(base + start, lanes)].astype(F32)
                ext[j, lead:] = buf[:, at].astype(F32)
                return (
                    taps[0:1] * ext[j, lead : lead + tok]
                    + taps[1:2] * ext[j, pl.ds(lead - 1, tok)]
                    + taps[2:3] * ext[j, pl.ds(lead - 2, tok)]
                )

            gated = featurized(k_buf, k_ext, width) * featurized(v_buf, v_ext, 2 * width)
            gated = gated.astype(BF16).T.astype(F32)
            taken = f_buf[:, at].T.astype(F32)
            e_ext[j, 0:2] = k_ext[j, lead : lead + 2]
            e_ext[j, 2:4] = v_ext[j, lead : lead + 2]
            e_ext[j, 4:6] = k_ext[j, lead + tok - 2 : lead + tok]
            e_ext[j, 6:8] = v_ext[j, lead + tok - 2 : lead + tok]
            edge = e_ext[j]
            turned = edge
            for m in range(1, near):
                turned = jnp.where(row == m, pltpu.roll(edge, m * own, 1), turned)
            for k in range(near):
                to = (j * near + k) * run
                mine = slice(k * own, (k + 1) * own)
                stage[to : to + own, :] = gated[mine]
                stage[to + own : to + 2 * own, :] = taken[mine]
                part = pltpu.roll(turned, lanes - k * own, 1) if k else turned
                part = jnp.where(row == piece, part, 0.0)
                part = part + pltpu.roll(part, 7, 0)
                part = part + pltpu.roll(part, 6, 0)
                stage[to + 2 * own : to + 2 * own + 1, :] = part[0:1]
                stage[to + 2 * own + 1 : to + 2 * own + 2, :] = part[4:5]
        out_buf[pl.ds(pl.multiple_of(i * chunk, chunk), chunk), :] = stage[...].astype(BF16)
        write(i).start()
        return carry

    lax.fori_loop(0, steps, turn, 0)

    def drain(i, carry):
        write(i).wait()
        return carry

    lax.fori_loop(0, steps, drain, 0)


def gate(projected, short_filter, long_filter, devices):
    tok, width = long_filter.shape
    own = width // devices
    steps = 8
    cols = width // steps
    run = 2 * own + EXTRA
    return pl.pallas_call(
        functools.partial(gate_kernel, own),
        in_specs=[pl.BlockSpec(memory_space=pltpu.HBM)] * 3,
        out_specs=pl.BlockSpec(memory_space=pltpu.HBM),
        out_shape=pltpu.HBM((devices * run, tok), BF16),
        scratch_shapes=[
            pltpu.VMEM(short_filter.shape, BF16),
            pltpu.VMEM((tok, width), BF16),
            pltpu.VMEM((tok, width), BF16),
            pltpu.VMEM((tok, width), BF16),
            pltpu.VMEM((devices * run, tok), BF16),
            pltpu.VMEM((cols // 128, tok + 8, 128), F32),
            pltpu.VMEM((cols // 128, tok + 8, 128), F32),
            pltpu.VMEM((cols // 128, 8, 128), F32),
            pltpu.VMEM((cols // own * run, 128), F32),
            pltpu.SemaphoreType.DMA((steps, 4)),
            pltpu.SemaphoreType.DMA(()),
        ],
        compiler_params=pltpu.CompilerParams(vmem_limit_bytes=20 << 20),
        name="gate",
    )(in_hbm(projected), in_hbm(long_filter), in_hbm(short_filter))


def dot(a, b):
    return jnp.dot(a, b, preferred_element_type=F32)


def spectral_kernel(
    outer, z_ref, taps_ref, first_ref, fwd_ref, bwd_ref, last_ref, tc_ref, ts_ref, hc_ref, hs_ref,
    out_ref, rows_ref, fix_ref, spec_ref, half_ref, half_out_ref, prod_ref, back_ref, conv_ref, block_ref, sem,
):
    segments, own, tok = out_ref.shape
    both = 2 * own
    pitch = both + EXTRA
    out_pitch = conv_ref.shape[0] // segments
    piece = 16
    rim = outer * pitch

    def widen(i, carry):
        start = pl.multiple_of(i * (piece * pitch), piece * pitch)
        block = z_ref[pl.ds(start, piece * pitch), :].astype(F32)
        rows_ref[pl.ds(rim + start, piece * pitch), :] = block
        return carry

    lax.fori_loop(0, segments // piece, widen, 0)

    rows_ref[pitch - 1 : pitch, :] = jnp.zeros((1, tok), F32)
    for o in range(1, outer):
        last = (segments + o - 1) * pitch + pitch - 1
        rows_ref[o * pitch + pitch - 1 : (o + 1) * pitch, :] = rows_ref[last : last + 1, :]
    now = rows_ref[pl.ds(rim + both, segments, stride=pitch), :]
    ago = rows_ref[pl.ds(both + 1, segments, stride=pitch), :]
    lane = lax.broadcasted_iota(jnp.int32, (segments, tok), 1)
    middle = jnp.where(
        lane // own % 2 == 0, pltpu.roll(ago, tok - own, 1), pltpu.roll(now, own, 1)
    )
    edges = taps_ref[0:1, :] * now + taps_ref[1:2, :] * middle + taps_ref[2:3, :] * ago
    edges = edges * pltpu.roll(edges, tok - 2 * own, 1)
    after = pltpu.roll(edges, tok - own + 1, 1)
    fix_ref[0] = jnp.where(lane % 2 == 0, edges, after)
    fix_ref[1] = jnp.where(lane % 2 == 1, edges, after)

    top = 8
    index = lax.broadcasted_iota(jnp.int32, (top, tok), 0)

    def first_row(row, block):
        return jnp.concatenate([jnp.where(index == 0, row, block[:top]), block[top:]], 0)

    group, group2, group3, group4 = 16, 16, 16, 16

    run = 16

    def first_section(which, i, carry):
        start = i * group
        base = which * own + start
        cols = []
        for j in range(group):
            col = rows_ref[pl.ds(rim + base + j, segments, stride=pitch), :]
            if which == 0:
                fixed = pltpu.roll(fix_ref[j % 2], (tok - start - j) % tok, 1)
                col = jnp.where(lane < 2, fixed, col)
            cols.append(col.astype(BF16))
        out = dot(first_ref[...], jnp.concatenate(cols, 1))
        out = out.reshape(segments // top, 2, top, group * tok)
        tc, ts = tc_ref[...], ts_ref[...]
        for j in range(group):
            real = out[:, 0, :, j * tok : (j + 1) * tok].reshape(segments, tok)
            imag = out[:, 1, :, j * tok : (j + 1) * tok].reshape(segments, tok)
            half_ref[pl.ds(base + j, 1), :] = imag[0:1]
            imag = first_row(0.0, imag)
            both_parts = jnp.concatenate([real * tc + imag * ts, imag * tc - real * ts], 1)
            both_parts = both_parts.astype(BF16).reshape(segments // run, run, 2 * tok)
            spec_ref[start + j, :, which] = both_parts
        return carry

    for which in range(2):
        lax.fori_loop(0, own // group, functools.partial(first_section, which), 0)

    def product(sig, fil):
        sr, si, fr, fi = sig[:, :tok], sig[:, tok:], fil[:, :tok], fil[:, tok:]
        return jnp.concatenate(
            [(sr * fr - si * fi).astype(BF16), (sr * fi + si * fr).astype(BF16)], 1
        )

    half = half_ref[...]
    hc, hs = hc_ref[...], hs_ref[...]
    half = jnp.concatenate([(half * hc).astype(BF16), (-half * hs).astype(BF16)], 1)
    half = dot(half, fwd_ref[...])
    half = dot(product(half[:own], half[own:]), bwd_ref[...])
    half_out_ref[...] = half[:, :tok] * hc - half[:, tok:] * hs

    def multiply(i, carry):
        start = i * group2
        spec = spec_ref[pl.ds(start, group2)].reshape(group2 * 2 * segments, 2 * tok)
        spec = dot(spec, fwd_ref[...]).reshape(group2 * segments // run, 2, run, 2 * tok)
        sig = spec[:, 0].reshape(group2 * segments, 2 * tok)
        fil = spec[:, 1].reshape(group2 * segments, 2 * tok)
        prod_ref[pl.ds(start, group2)] = product(sig, fil).reshape(group2, segments, 2 * tok)
        return carry

    lax.fori_loop(0, own // group2, multiply, 0)

    def invert(i, carry):
        start = i * group3
        tc, ts = tc_ref[...], ts_ref[...]
        back = dot(
            prod_ref[pl.ds(start, group3)].reshape(group3 * segments, 2 * tok), bwd_ref[...]
        )
        for j in range(group3):
            br = back[j * segments : (j + 1) * segments, :tok]
            bi = back[j * segments : (j + 1) * segments, tok:]
            imag = first_row(half_out_ref[pl.ds(start + j, 1), :], bi * tc + br * ts)
            back_ref[start + j, :segments] = (br * tc - bi * ts).astype(BF16)
            back_ref[start + j, segments:] = imag.astype(BF16)
        return carry

    lax.fori_loop(0, own // group3, invert, 0)

    def finish(i, carry):
        start = i * group4
        stacked = jnp.concatenate([back_ref[start + j] for j in range(group4)], 1)
        conv = dot(last_ref[...], stacked)
        for j in range(group4):
            conv_ref[pl.ds(start + j, segments, stride=out_pitch), :] = conv[
                :, j * tok : (j + 1) * tok
            ]
        return carry

    lax.fori_loop(0, own // group4, finish, 0)

    def write(i):
        at = pl.ds(i * piece, piece)
        return pltpu.make_async_copy(block_ref.at[at], out_ref.at[at], sem.at[i])

    def narrow(i, carry):
        for j in range(piece):
            b = i * piece + j
            block_ref[b] = conv_ref[pl.ds(b * out_pitch, own), :].astype(BF16)
        write(i).start()
        return carry

    lax.fori_loop(0, segments // piece, narrow, 0)
    for i in range(segments // piece):
        write(i).wait()


def spectral(received, taps, consts, outer, own):
    tok = received.shape[1]
    both = 2 * own
    pitch = both + EXTRA
    segments = received.shape[0] // pitch
    return pl.pallas_call(
        functools.partial(spectral_kernel, outer),
        out_shape=pltpu.HBM((segments, own, tok), BF16),
        in_specs=[pl.BlockSpec(memory_space=pltpu.VMEM)] * 10,
        out_specs=pl.BlockSpec(memory_space=pltpu.HBM),
        scratch_shapes=[
            pltpu.VMEM(((segments + outer) * pitch, tok), F32),
            pltpu.VMEM((2, segments, tok), F32),
            pltpu.VMEM((own, segments // 16, 2, 16, 2 * tok), BF16),
            pltpu.VMEM((both, tok), F32),
            pltpu.VMEM((own, tok), F32),
            pltpu.VMEM((own, segments, 2 * tok), BF16),
            pltpu.VMEM((own, 2 * segments, tok), BF16),
            pltpu.VMEM((segments * (own + PAD), tok), F32),
            pltpu.VMEM((segments, own, tok), BF16),
            pltpu.SemaphoreType.DMA((segments // 16,)),
        ],
        compiler_params=pltpu.CompilerParams(vmem_limit_bytes=28 << 20),
        name="spectral",
    )(resident(received), taps, *consts)


def mix_kernel(c_ref, q_ref, skip_ref, g_ref, out_ref, buf_ref, sem):
    peers, own, tok = c_ref.shape
    steps = sem.shape[0]
    peers = peers // steps
    cols = peers * own
    near = 128 // own

    def write(i):
        at = pl.ds(i * cols, cols)
        return pltpu.make_async_copy(buf_ref.at[:, at], out_ref.at[:, at], sem.at[i])

    for i in range(steps):
        for j in range(i * peers, (i + 1) * peers, near):
            at = slice(j * own, (j + near) * own)
            conv = c_ref[j : j + near].reshape(near * own, tok).T.astype(F32)
            direct = skip_ref[:, at] * g_ref[:, at].astype(F32)
            buf_ref[:, at] = (q_ref[:, at].astype(F32) * (conv + direct)).astype(BF16)
        write(i).start()
    for i in range(steps):
        write(i).wait()


def resident(value):
    return pltpu.with_memory_space_constraint(value, pltpu.VMEM)


def mix(conv, query, skip, gated):
    devices, own, tok = conv.shape
    width = devices * own
    steps = 8
    return pl.pallas_call(
        mix_kernel,
        in_specs=[pl.BlockSpec(memory_space=pltpu.VMEM)] * 4,
        out_specs=pl.BlockSpec(memory_space=pltpu.HBM),
        out_shape=jax.ShapeDtypeStruct((tok, width), BF16),
        scratch_shapes=[
            pltpu.VMEM((tok, width), BF16),
            pltpu.SemaphoreType.DMA((steps,)),
        ],
        compiler_params=pltpu.CompilerParams(vmem_limit_bytes=6 << 20),
        name="mix",
    )(resident(conv), resident(query), resident(skip), resident(gated))


def side_kernel(q_ref, k_ref, v_ref, rq_ref, rk_ref, rv_ref, wq_ref, wk_ref, wv_ref,
                query_ref, gated_ref):
    def featurized(rows_ref, rim_ref, taps_ref):
        rows = rows_ref[...].astype(F32)
        rim = rim_ref[...].astype(F32)
        taps = taps_ref[...].astype(F32)
        index = lax.broadcasted_iota(jnp.int32, rows.shape, 0)
        back1 = jnp.where(index == 0, rim[1:2], pltpu.roll(rows, 1, 0))
        back2 = pltpu.roll(rows, 2, 0)
        back2 = jnp.where(index == 0, rim[0:1], jnp.where(index == 1, rim[1:2], back2))
        return taps[0:1] * rows + taps[1:2] * back1 + taps[2:3] * back2

    query_ref[...] = featurized(q_ref, rq_ref, wq_ref).astype(BF16)
    gated = featurized(k_ref, rk_ref, wk_ref) * featurized(v_ref, rv_ref, wv_ref)
    gated_ref[...] = gated.astype(BF16)


def side(projected, rim, short_filter):
    tok = projected.shape[0]
    width = projected.shape[1] // 3
    steps = 8
    cols = width // steps

    def thirds(rows):
        return [
            pl.BlockSpec((rows, cols), functools.partial(lambda third, i: (0, i + third * steps), t))
            for t in range(3)
        ]

    wide = pl.BlockSpec((tok, cols), lambda i: (0, i))
    return pl.pallas_call(
        side_kernel,
        grid=(steps,),
        in_specs=thirds(tok)
        + thirds(rim.shape[0])
        + thirds(short_filter.shape[0]),
        out_specs=[wide, wide],
        out_shape=[
            jax.ShapeDtypeStruct((tok, width), BF16),
            jax.ShapeDtypeStruct((tok, width), BF16),
        ],
        compiler_params=pltpu.CompilerParams(vmem_limit_bytes=8 << 20),
        name="side",
    )(*[in_hbm(projected)] * 3, *[rim] * 3, *[short_filter] * 3)


def shards(projected, short_filter, long_filter, skip):
    devices = lax.axis_size(AXES)
    tok, width = long_filter.shape
    own = width // devices
    tap_count = short_filter.shape[0]
    rim_count = tap_count - 1
    outer = lax.axis_size("outer")
    order = np.arange(devices).reshape(outer, -1).T.reshape(-1)
    consts = tables(order, tok)
    position = lax.axis_index(TURNED)
    taps = [
        lax.dynamic_slice_in_dim(short_filter, third * width + position * own, own, 1)
        for third in (1, 2)
    ]
    taps = jnp.concatenate([taps[0], taps[0], taps[1], taps[1]], 1).astype(F32)
    send = gate(projected, short_filter, long_filter, devices)
    pairs = send.reshape(devices, -1, 2, tok)
    received = lax.all_to_all(pairs, TURNED, split_axis=0, concat_axis=0, tiled=True)
    received = received.reshape(send.shape)
    rim = lax.ppermute(projected[tok - rim_count :], AXES, [(i, i + 1) for i in range(devices - 1)])
    query, gated = side(projected, rim, short_filter)
    conv = spectral(received, taps, consts, outer, own)
    conv = lax.all_to_all(conv, TURNED, split_axis=0, concat_axis=0, tiled=True)
    return mix(conv, query, skip[None, :], gated)


def solution(mesh):
    in_specs = (P(AXES, None), P(), P(AXES, None), P())
    return jax.shard_map(
        shards, mesh=mesh, in_specs=in_specs, out_specs=P(AXES, None), check_vma=False
    )
```

```python
import functools
import math

import jax
import jax.numpy as jnp
import numpy as np
from jax import lax
from jax.experimental import pallas as pl
from jax.experimental.pallas import tpu as pltpu
from jax.sharding import PartitionSpec as P


AXES = ("outer", "inner")
TURNED = ("inner", "outer")
F32 = jnp.float32
BF16 = jnp.bfloat16
PAD = 1


def turn_table(rows, cols, length):
    product = (np.asarray(rows, np.int64) * np.asarray(cols, np.int64)) % length
    angle = product.astype(np.float32) * np.float32(2.0 * math.pi / length)
    angle = angle.astype(np.float64)
    return np.cos(angle).astype(np.float32), np.sin(angle).astype(np.float32)


def paired(reals, imags):
    both = np.stack([reals.reshape(-1, 8, reals.shape[1]), imags.reshape(-1, 8, imags.shape[1])], 1)
    return both.reshape(-1, reals.shape[1])


def tables(order, tok):
    segments = len(order)
    half = segments
    blocks = 2 * segments
    transform = blocks * tok
    kb = np.arange(half + 1)
    cos_b, sin_b = turn_table(kb[:, None], np.asarray(order)[None, :], blocks)
    first = paired(cos_b[:half], np.concatenate([cos_b[half:], -sin_b[1:half]], 0))
    weight = np.full((half + 1,), 2.0, np.float32)
    weight[0] = weight[half] = 1.0
    cos_w = cos_b.astype(BF16).astype(np.float32) * weight[:, None]
    sin_w = sin_b.astype(BF16).astype(np.float32) * weight[:, None]
    last = np.concatenate([cos_w[:half], cos_w[half:], -sin_w[1:half]], 0).T / transform
    cos_l, sin_l = turn_table(np.arange(tok)[:, None], np.arange(tok)[None, :], tok)
    forward = np.block([[cos_l, -sin_l], [sin_l, cos_l]])
    backward = np.block([[cos_l, sin_l], [-sin_l, cos_l]])
    turn_cos, turn_sin = turn_table(kb[:, None], np.arange(tok)[None, :], transform)
    return (
        first.astype(BF16),
        forward.astype(BF16),
        backward.astype(BF16),
        last.astype(BF16),
        turn_cos[:half],
        turn_sin[:half],
        turn_cos[half:],
        turn_sin[half:],
    )


EXTRA = 2


def in_hbm(value):
    return pltpu.with_memory_space_constraint(value, pltpu.HBM)


def gate_kernel(
    own, p_ref, f_ref, t_ref, send_ref, w_ref, k_buf, v_buf, f_buf, out_buf, k_ext, v_ext, e_ext,
    stage, sem, tap_sem,
):
    tok, width = f_ref.shape
    run = 2 * own + EXTRA
    steps = sem.shape[0]
    cols = width // steps
    lanes = e_ext.shape[2]
    near = lanes // own
    chunk = cols // own * run
    ahead = 2

    def reads(i):
        start = pl.multiple_of(i * cols, cols)
        at = pl.ds(start, cols)
        return (
            pltpu.make_async_copy(
                p_ref.at[:, pl.ds(width + start, cols)], k_buf.at[:, at], sem.at[i, 0]
            ),
            pltpu.make_async_copy(
                p_ref.at[:, pl.ds(2 * width + start, cols)], v_buf.at[:, at], sem.at[i, 1]
            ),
            pltpu.make_async_copy(f_ref.at[:, at], f_buf.at[:, at], sem.at[i, 2]),
        )

    def write(i):
        at = pl.ds(pl.multiple_of(i * chunk, chunk), chunk)
        return pltpu.make_async_copy(out_buf.at[at], send_ref.at[at], sem.at[i, 3])

    taps_read = pltpu.make_async_copy(t_ref, w_ref, tap_sem)
    taps_read.start()
    for i in range(ahead):
        for copy in reads(i):
            copy.start()
    lead = 8
    for j in range(cols // lanes):
        k_ext[j, :lead] = jnp.zeros((lead, lanes), F32)
        v_ext[j, :lead] = jnp.zeros((lead, lanes), F32)
    row = lax.broadcasted_iota(jnp.int32, (8, lanes), 0) % 4
    piece = lax.broadcasted_iota(jnp.int32, (8, lanes), 1) // own
    square = (lanes, lanes)
    one = lax.broadcasted_iota(jnp.int32, square, 0) == lax.broadcasted_iota(jnp.int32, square, 1)
    one = one.astype(F32).astype(BF16)
    taps_read.wait()

    def turn(i, carry):
        for copy in reads(i):
            copy.wait()

        @pl.when(i + ahead < steps)
        def _():
            for copy in reads(i + ahead):
                copy.start()

        for j in range(cols // lanes):
            start = pl.multiple_of(i * cols + j * lanes, lanes)
            at = pl.ds(start, lanes)

            def featurized(buf, ext, base):
                taps = w_ref[:, pl.ds(base + start, lanes)].astype(F32)
                ext[j, lead:] = buf[:, at].astype(F32)
                return (
                    taps[0:1] * ext[j, lead : lead + tok]
                    + taps[1:2] * ext[j, pl.ds(lead - 1, tok)]
                    + taps[2:3] * ext[j, pl.ds(lead - 2, tok)]
                )

            gated = featurized(k_buf, k_ext, width) * featurized(v_buf, v_ext, 2 * width)
            both = jnp.concatenate([gated.astype(BF16), f_buf[:, at]], 0)
            both = lax.dot_general(
                one, both, (((1,), (1,)), ((), ())), preferred_element_type=F32
            )
            gated, taken = both[:, :tok], both[:, tok:]
            e_ext[j, 0:2] = k_ext[j, lead : lead + 2]
            e_ext[j, 2:4] = v_ext[j, lead : lead + 2]
            e_ext[j, 4:6] = k_ext[j, lead + tok - 2 : lead + tok]
            e_ext[j, 6:8] = v_ext[j, lead + tok - 2 : lead + tok]
            edge = e_ext[j]
            turned = edge
            for m in range(1, near):
                turned = jnp.where(row == m, pltpu.roll(edge, m * own, 1), turned)
            for k in range(near):
                to = (j * near + k) * run
                mine = slice(k * own, (k + 1) * own)
                stage[to : to + own, :] = gated[mine]
                stage[to + own : to + 2 * own, :] = taken[mine]
                part = pltpu.roll(turned, lanes - k * own, 1) if k else turned
                part = jnp.where(row == piece, part, 0.0)
                part = part + pltpu.roll(part, 7, 0)
                part = part + pltpu.roll(part, 6, 0)
                stage[to + 2 * own : to + 2 * own + 1, :] = part[0:1]
                stage[to + 2 * own + 1 : to + 2 * own + 2, :] = part[4:5]
        out_buf[pl.ds(pl.multiple_of(i * chunk, chunk), chunk), :] = stage[...].astype(BF16)
        write(i).start()
        return carry

    lax.fori_loop(0, steps, turn, 0)

    def drain(i, carry):
        write(i).wait()
        return carry

    lax.fori_loop(0, steps, drain, 0)


def gate(projected, short_filter, long_filter, devices):
    tok, width = long_filter.shape
    own = width // devices
    steps = 4
    cols = width // steps
    run = 2 * own + EXTRA
    return pl.pallas_call(
        functools.partial(gate_kernel, own),
        in_specs=[pl.BlockSpec(memory_space=pltpu.HBM)] * 3,
        out_specs=pl.BlockSpec(memory_space=pltpu.HBM),
        out_shape=pltpu.HBM((devices * run, tok), BF16),
        scratch_shapes=[
            pltpu.VMEM(short_filter.shape, BF16),
            pltpu.VMEM((tok, width), BF16),
            pltpu.VMEM((tok, width), BF16),
            pltpu.VMEM((tok, width), BF16),
            pltpu.VMEM((devices * run, tok), BF16),
            pltpu.VMEM((cols // 128, tok + 8, 128), F32),
            pltpu.VMEM((cols // 128, tok + 8, 128), F32),
            pltpu.VMEM((cols // 128, 8, 128), F32),
            pltpu.VMEM((cols // own * run, 128), F32),
            pltpu.SemaphoreType.DMA((steps, 4)),
            pltpu.SemaphoreType.DMA(()),
        ],
        compiler_params=pltpu.CompilerParams(vmem_limit_bytes=20 << 20),
        name="gate",
    )(in_hbm(projected), in_hbm(long_filter), in_hbm(short_filter))


def dot(a, b):
    return jnp.dot(a, b, preferred_element_type=F32)


def spectral_kernel(
    outer, z_ref, taps_ref, first_ref, fwd_ref, bwd_ref, last_ref, tc_ref, ts_ref, hc_ref, hs_ref,
    out_ref, rows_ref, fix_ref, spec_ref, half_ref, half_out_ref, prod_ref, back_ref, conv_ref, block_ref, sem,
):
    segments, own, tok = out_ref.shape
    both = 2 * own
    pitch = both + EXTRA
    out_pitch = conv_ref.shape[0] // segments
    piece = 16
    rim = outer * pitch

    def widen(i, carry):
        start = pl.multiple_of(i * (piece * pitch), piece * pitch)
        block = z_ref[pl.ds(start, piece * pitch), :].astype(F32)
        rows_ref[pl.ds(rim + start, piece * pitch), :] = block
        return carry

    lax.fori_loop(0, segments // piece, widen, 0)

    rows_ref[pitch - 1 : pitch, :] = jnp.zeros((1, tok), F32)
    for o in range(1, outer):
        last = (segments + o - 1) * pitch + pitch - 1
        rows_ref[o * pitch + pitch - 1 : (o + 1) * pitch, :] = rows_ref[last : last + 1, :]
    now = rows_ref[pl.ds(rim + both, segments, stride=pitch), :]
    ago = rows_ref[pl.ds(both + 1, segments, stride=pitch), :]
    lane = lax.broadcasted_iota(jnp.int32, (segments, tok), 1)
    middle = jnp.where(
        lane // own % 2 == 0, pltpu.roll(ago, tok - own, 1), pltpu.roll(now, own, 1)
    )
    edges = taps_ref[0:1, :] * now + taps_ref[1:2, :] * middle + taps_ref[2:3, :] * ago
    edges = edges * pltpu.roll(edges, tok - 2 * own, 1)
    after = pltpu.roll(edges, tok - own + 1, 1)
    fix_ref[0] = jnp.where(lane % 2 == 0, edges, after)
    fix_ref[1] = jnp.where(lane % 2 == 1, edges, after)

    top = 8
    index = lax.broadcasted_iota(jnp.int32, (top, tok), 0)

    def first_row(row, block):
        return jnp.concatenate([jnp.where(index == 0, row, block[:top]), block[top:]], 0)

    group, group2, group3, group4 = 16, 16, 16, 16

    run = 16

    def first_section(which, i, carry):
        start = i * group
        base = which * own + start
        cols = []
        for j in range(group):
            col = rows_ref[pl.ds(rim + base + j, segments, stride=pitch), :]
            if which == 0:
                fixed = pltpu.roll(fix_ref[j % 2], (tok - start - j) % tok, 1)
                col = jnp.where(lane < 2, fixed, col)
            cols.append(col.astype(BF16))
        out = dot(first_ref[...], jnp.concatenate(cols, 1))
        out = out.reshape(segments // top, 2, top, group * tok)
        tc, ts = tc_ref[...], ts_ref[...]
        for j in range(group):
            real = out[:, 0, :, j * tok : (j + 1) * tok].reshape(segments, tok)
            imag = out[:, 1, :, j * tok : (j + 1) * tok].reshape(segments, tok)
            half_ref[pl.ds(base + j, 1), :] = imag[0:1]
            imag = first_row(0.0, imag)
            both_parts = jnp.concatenate([real * tc + imag * ts, imag * tc - real * ts], 1)
            both_parts = both_parts.astype(BF16).reshape(segments // run, run, 2 * tok)
            spec_ref[start + j, :, which] = both_parts
        return carry

    for which in range(2):
        lax.fori_loop(0, own // group, functools.partial(first_section, which), 0)

    def product(sig, fil):
        sr, si, fr, fi = sig[:, :tok], sig[:, tok:], fil[:, :tok], fil[:, tok:]
        return jnp.concatenate(
            [(sr * fr - si * fi).astype(BF16), (sr * fi + si * fr).astype(BF16)], 1
        )

    half = half_ref[...]
    hc, hs = hc_ref[...], hs_ref[...]
    half = jnp.concatenate([(half * hc).astype(BF16), (-half * hs).astype(BF16)], 1)
    half = dot(half, fwd_ref[...])
    half = dot(product(half[:own], half[own:]), bwd_ref[...])
    half_out_ref[...] = half[:, :tok] * hc - half[:, tok:] * hs

    def multiply(i, carry):
        start = i * group2
        spec = spec_ref[pl.ds(start, group2)].reshape(group2 * 2 * segments, 2 * tok)
        spec = dot(spec, fwd_ref[...]).reshape(group2 * segments // run, 2, run, 2 * tok)
        sig = spec[:, 0].reshape(group2 * segments, 2 * tok)
        fil = spec[:, 1].reshape(group2 * segments, 2 * tok)
        prod_ref[pl.ds(start, group2)] = product(sig, fil).reshape(group2, segments, 2 * tok)
        return carry

    lax.fori_loop(0, own // group2, multiply, 0)

    def invert(i, carry):
        start = i * group3
        tc, ts = tc_ref[...], ts_ref[...]
        back = dot(
            prod_ref[pl.ds(start, group3)].reshape(group3 * segments, 2 * tok), bwd_ref[...]
        )
        for j in range(group3):
            br = back[j * segments : (j + 1) * segments, :tok]
            bi = back[j * segments : (j + 1) * segments, tok:]
            imag = first_row(half_out_ref[pl.ds(start + j, 1), :], bi * tc + br * ts)
            back_ref[start + j, :segments] = (br * tc - bi * ts).astype(BF16)
            back_ref[start + j, segments:] = imag.astype(BF16)
        return carry

    lax.fori_loop(0, own // group3, invert, 0)

    def finish(i, carry):
        start = i * group4
        stacked = jnp.concatenate([back_ref[start + j] for j in range(group4)], 1)
        conv = dot(last_ref[...], stacked)
        for j in range(group4):
            conv_ref[pl.ds(start + j, segments, stride=out_pitch), :] = conv[
                :, j * tok : (j + 1) * tok
            ]
        return carry

    def write(i):
        at = pl.ds(pl.multiple_of(i * group4, group4), group4)
        return pltpu.make_async_copy(block_ref.at[:, at], out_ref.at[:, at], sem.at[i])

    def finish_and_send(i, carry):
        finish(i, carry)
        start = pl.multiple_of(i * group4, group4)

        def narrow(n, inner):
            for j in range(piece):
                b = n * piece + j
                rows = conv_ref[pl.ds(b * out_pitch + start, group4), :]
                block_ref[b, pl.ds(start, group4), :] = rows.astype(BF16)
            return inner

        lax.fori_loop(0, segments // piece, narrow, 0)
        write(i).start()
        return carry

    lax.fori_loop(0, own // group4, finish_and_send, 0)
    for i in range(own // group4):
        write(i).wait()


def spectral(received, taps, consts, outer, own):
    tok = received.shape[1]
    both = 2 * own
    pitch = both + EXTRA
    segments = received.shape[0] // pitch
    return pl.pallas_call(
        functools.partial(spectral_kernel, outer),
        out_shape=pltpu.HBM((segments, own, tok), BF16),
        in_specs=[pl.BlockSpec(memory_space=pltpu.VMEM)] * 10,
        out_specs=pl.BlockSpec(memory_space=pltpu.HBM),
        scratch_shapes=[
            pltpu.VMEM(((segments + outer) * pitch, tok), F32),
            pltpu.VMEM((2, segments, tok), F32),
            pltpu.VMEM((own, segments // 16, 2, 16, 2 * tok), BF16),
            pltpu.VMEM((both, tok), F32),
            pltpu.VMEM((own, tok), F32),
            pltpu.VMEM((own, segments, 2 * tok), BF16),
            pltpu.VMEM((own, 2 * segments, tok), BF16),
            pltpu.VMEM((segments * (own + PAD), tok), F32),
            pltpu.VMEM((segments, own, tok), BF16),
            pltpu.SemaphoreType.DMA((segments // 16,)),
        ],
        compiler_params=pltpu.CompilerParams(vmem_limit_bytes=28 << 20),
        name="spectral",
    )(resident(received), taps, *consts)


def mix_kernel(c_ref, q_ref, skip_ref, g_ref, out_ref, buf_ref, sem):
    peers, own, tok = c_ref.shape
    steps = sem.shape[0]
    peers = peers // steps
    cols = peers * own
    near = 128 // own

    def write(i):
        at = pl.ds(i * cols, cols)
        return pltpu.make_async_copy(buf_ref.at[:, at], out_ref.at[:, at], sem.at[i])

    for i in range(steps):
        for j in range(i * peers, (i + 1) * peers, near):
            at = slice(j * own, (j + near) * own)
            conv = c_ref[j : j + near].reshape(near * own, tok).T.astype(F32)
            direct = skip_ref[:, at] * g_ref[:, at].astype(F32)
            buf_ref[:, at] = (q_ref[:, at].astype(F32) * (conv + direct)).astype(BF16)
        write(i).start()
    for i in range(steps):
        write(i).wait()


def resident(value):
    return pltpu.with_memory_space_constraint(value, pltpu.VMEM)


def mix(conv, query, skip, gated):
    devices, own, tok = conv.shape
    width = devices * own
    steps = 8
    return pl.pallas_call(
        mix_kernel,
        in_specs=[pl.BlockSpec(memory_space=pltpu.VMEM)] * 4,
        out_specs=pl.BlockSpec(memory_space=pltpu.HBM),
        out_shape=jax.ShapeDtypeStruct((tok, width), BF16),
        scratch_shapes=[
            pltpu.VMEM((tok, width), BF16),
            pltpu.SemaphoreType.DMA((steps,)),
        ],
        compiler_params=pltpu.CompilerParams(vmem_limit_bytes=6 << 20),
        name="mix",
    )(resident(conv), resident(query), resident(skip), resident(gated))


def side_kernel(q_ref, k_ref, v_ref, rq_ref, rk_ref, rv_ref, wq_ref, wk_ref, wv_ref,
                query_ref, gated_ref):
    def featurized(rows_ref, rim_ref, taps_ref):
        rows = rows_ref[...].astype(F32)
        rim = rim_ref[...].astype(F32)
        taps = taps_ref[...].astype(F32)
        index = lax.broadcasted_iota(jnp.int32, rows.shape, 0)
        back1 = jnp.where(index == 0, rim[1:2], pltpu.roll(rows, 1, 0))
        back2 = pltpu.roll(rows, 2, 0)
        back2 = jnp.where(index == 0, rim[0:1], jnp.where(index == 1, rim[1:2], back2))
        return taps[0:1] * rows + taps[1:2] * back1 + taps[2:3] * back2

    query_ref[...] = featurized(q_ref, rq_ref, wq_ref).astype(BF16)
    gated = featurized(k_ref, rk_ref, wk_ref) * featurized(v_ref, rv_ref, wv_ref)
    gated_ref[...] = gated.astype(BF16)


def side(projected, rim, short_filter):
    tok = projected.shape[0]
    width = projected.shape[1] // 3
    steps = 8
    cols = width // steps

    def thirds(rows):
        return [
            pl.BlockSpec((rows, cols), functools.partial(lambda third, i: (0, i + third * steps), t))
            for t in range(3)
        ]

    wide = pl.BlockSpec((tok, cols), lambda i: (0, i))
    return pl.pallas_call(
        side_kernel,
        grid=(steps,),
        in_specs=thirds(tok)
        + thirds(rim.shape[0])
        + thirds(short_filter.shape[0]),
        out_specs=[wide, wide],
        out_shape=[
            jax.ShapeDtypeStruct((tok, width), BF16),
            jax.ShapeDtypeStruct((tok, width), BF16),
        ],
        compiler_params=pltpu.CompilerParams(vmem_limit_bytes=8 << 20),
        name="side",
    )(*[in_hbm(projected)] * 3, *[rim] * 3, *[short_filter] * 3)


def shards(projected, short_filter, long_filter, skip):
    devices = lax.axis_size(AXES)
    tok, width = long_filter.shape
    own = width // devices
    tap_count = short_filter.shape[0]
    rim_count = tap_count - 1
    outer = lax.axis_size("outer")
    order = np.arange(devices).reshape(outer, -1).T.reshape(-1)
    consts = tables(order, tok)
    position = lax.axis_index(TURNED)
    taps = [
        lax.dynamic_slice_in_dim(short_filter, third * width + position * own, own, 1)
        for third in (1, 2)
    ]
    taps = jnp.concatenate([taps[0], taps[0], taps[1], taps[1]], 1).astype(F32)
    send = gate(projected, short_filter, long_filter, devices)
    pairs = send.reshape(devices, -1, 2, tok)
    received = lax.all_to_all(pairs, TURNED, split_axis=0, concat_axis=0, tiled=True)
    received = received.reshape(send.shape)
    rim = lax.ppermute(projected[tok - rim_count :], AXES, [(i, i + 1) for i in range(devices - 1)])
    query, gated = side(projected, rim, short_filter)
    conv = spectral(received, taps, consts, outer, own)
    conv = lax.all_to_all(conv, TURNED, split_axis=0, concat_axis=0, tiled=True)
    return mix(conv, query, skip[None, :], gated)


def solution(mesh):
    in_specs = (P(AXES, None), P(), P(AXES, None), P())
    return jax.shard_map(
        shards, mesh=mesh, in_specs=in_specs, out_specs=P(AXES, None), check_vma=False
    )
```

```python
import functools
import math

import jax
import jax.numpy as jnp
import numpy as np
from jax import lax
from jax.experimental import pallas as pl
from jax.experimental.pallas import tpu as pltpu
from jax.sharding import PartitionSpec as P


AXES = ("outer", "inner")
TURNED = ("inner", "outer")
F32 = jnp.float32
BF16 = jnp.bfloat16
PAD = 1


def turn_table(rows, cols, length):
    product = (np.asarray(rows, np.int64) * np.asarray(cols, np.int64)) % length
    angle = product.astype(np.float32) * np.float32(2.0 * math.pi / length)
    angle = angle.astype(np.float64)
    return np.cos(angle).astype(np.float32), np.sin(angle).astype(np.float32)


def paired(reals, imags):
    both = np.stack([reals.reshape(-1, 8, reals.shape[1]), imags.reshape(-1, 8, imags.shape[1])], 1)
    return both.reshape(-1, reals.shape[1])


def tables(order, tok):
    segments = len(order)
    half = segments
    blocks = 2 * segments
    transform = blocks * tok
    kb = np.arange(half + 1)
    cos_b, sin_b = turn_table(kb[:, None], np.asarray(order)[None, :], blocks)
    first = paired(cos_b[:half], np.concatenate([cos_b[half:], -sin_b[1:half]], 0))
    weight = np.full((half + 1,), 2.0, np.float32)
    weight[0] = weight[half] = 1.0
    cos_w = cos_b.astype(BF16).astype(np.float32) * weight[:, None]
    sin_w = sin_b.astype(BF16).astype(np.float32) * weight[:, None]
    last = np.concatenate([cos_w[:half], cos_w[half:], -sin_w[1:half]], 0).T / transform
    cos_l, sin_l = turn_table(np.arange(tok)[:, None], np.arange(tok)[None, :], tok)
    forward = np.block([[cos_l, -sin_l], [sin_l, cos_l]])
    backward = np.block([[cos_l, sin_l], [-sin_l, cos_l]])
    turn_cos, turn_sin = turn_table(kb[:, None], np.arange(tok)[None, :], transform)
    return (
        first.astype(BF16),
        forward.astype(BF16),
        backward.astype(BF16),
        last.astype(BF16),
        turn_cos[:half],
        turn_sin[:half],
        turn_cos[half:],
        turn_sin[half:],
    )


EXTRA = 2


def in_hbm(value):
    return pltpu.with_memory_space_constraint(value, pltpu.HBM)


def gate_kernel(
    own, p_ref, f_ref, t_ref, send_ref, w_ref, k_buf, v_buf, f_buf, out_buf, k_ext, v_ext, e_ext,
    stage, sem, tap_sem,
):
    tok, width = f_ref.shape
    run = 2 * own + EXTRA
    steps = sem.shape[0]
    cols = width // steps
    lanes = e_ext.shape[2]
    near = lanes // own
    chunk = cols // own * run
    ahead = 2

    def reads(i):
        start = pl.multiple_of(i * cols, cols)
        at = pl.ds(start, cols)
        return (
            pltpu.make_async_copy(
                p_ref.at[:, pl.ds(width + start, cols)], k_buf.at[:, at], sem.at[i, 0]
            ),
            pltpu.make_async_copy(
                p_ref.at[:, pl.ds(2 * width + start, cols)], v_buf.at[:, at], sem.at[i, 1]
            ),
            pltpu.make_async_copy(f_ref.at[:, at], f_buf.at[:, at], sem.at[i, 2]),
        )

    def write(i):
        at = pl.ds(pl.multiple_of(i * chunk, chunk), chunk)
        return pltpu.make_async_copy(out_buf.at[at], send_ref.at[at], sem.at[i, 3])

    taps_read = pltpu.make_async_copy(t_ref, w_ref, tap_sem)
    taps_read.start()
    for i in range(ahead):
        for copy in reads(i):
            copy.start()
    lead = 8
    for j in range(cols // lanes):
        k_ext[j, :lead] = jnp.zeros((lead, lanes), F32)
        v_ext[j, :lead] = jnp.zeros((lead, lanes), F32)
    row = lax.broadcasted_iota(jnp.int32, (8, lanes), 0) % 4
    piece = lax.broadcasted_iota(jnp.int32, (8, lanes), 1) // own
    square = (lanes, lanes)
    one = lax.broadcasted_iota(jnp.int32, square, 0) == lax.broadcasted_iota(jnp.int32, square, 1)
    one = one.astype(F32).astype(BF16)
    taps_read.wait()

    def turn(i, carry):
        for copy in reads(i):
            copy.wait()

        @pl.when(i + ahead < steps)
        def _():
            for copy in reads(i + ahead):
                copy.start()

        for j in range(cols // lanes):
            start = pl.multiple_of(i * cols + j * lanes, lanes)
            at = pl.ds(start, lanes)

            def featurized(buf, ext, base):
                taps = w_ref[:, pl.ds(base + start, lanes)].astype(F32)
                ext[j, lead:] = buf[:, at].astype(F32)
                return (
                    taps[0:1] * ext[j, lead : lead + tok]
                    + taps[1:2] * ext[j, pl.ds(lead - 1, tok)]
                    + taps[2:3] * ext[j, pl.ds(lead - 2, tok)]
                )

            gated = featurized(k_buf, k_ext, width) * featurized(v_buf, v_ext, 2 * width)
            both = jnp.concatenate([gated.astype(BF16), f_buf[:, at]], 0)
            both = lax.dot_general(
                one, both, (((1,), (1,)), ((), ())), preferred_element_type=F32
            )
            gated, taken = both[:, :tok], both[:, tok:]
            e_ext[j, 0:2] = k_ext[j, lead : lead + 2]
            e_ext[j, 2:4] = v_ext[j, lead : lead + 2]
            e_ext[j, 4:6] = k_ext[j, lead + tok - 2 : lead + tok]
            e_ext[j, 6:8] = v_ext[j, lead + tok - 2 : lead + tok]
            edge = e_ext[j]
            turned = edge
            for m in range(1, near):
                turned = jnp.where(row == m, pltpu.roll(edge, m * own, 1), turned)
            for k in range(near):
                to = (j * near + k) * run
                mine = slice(k * own, (k + 1) * own)
                stage[to : to + own, :] = gated[mine]
                stage[to + own : to + 2 * own, :] = taken[mine]
                part = pltpu.roll(turned, lanes - k * own, 1) if k else turned
                part = jnp.where(row == piece, part, 0.0)
                part = part + pltpu.roll(part, 7, 0)
                part = part + pltpu.roll(part, 6, 0)
                stage[to + 2 * own : to + 2 * own + 1, :] = part[0:1]
                stage[to + 2 * own + 1 : to + 2 * own + 2, :] = part[4:5]
        out_buf[pl.ds(pl.multiple_of(i * chunk, chunk), chunk), :] = stage[...].astype(BF16)
        write(i).start()
        return carry

    lax.fori_loop(0, steps, turn, 0)

    def drain(i, carry):
        write(i).wait()
        return carry

    lax.fori_loop(0, steps, drain, 0)


def gate(projected, short_filter, long_filter, devices):
    tok, width = long_filter.shape
    own = width // devices
    steps = 4
    cols = width // steps
    run = 2 * own + EXTRA
    return pl.pallas_call(
        functools.partial(gate_kernel, own),
        in_specs=[pl.BlockSpec(memory_space=pltpu.HBM)] * 3,
        out_specs=pl.BlockSpec(memory_space=pltpu.HBM),
        out_shape=pltpu.HBM((devices * run, tok), BF16),
        scratch_shapes=[
            pltpu.VMEM(short_filter.shape, BF16),
            pltpu.VMEM((tok, width), BF16),
            pltpu.VMEM((tok, width), BF16),
            pltpu.VMEM((tok, width), BF16),
            pltpu.VMEM((devices * run, tok), BF16),
            pltpu.VMEM((cols // 128, tok + 8, 128), F32),
            pltpu.VMEM((cols // 128, tok + 8, 128), F32),
            pltpu.VMEM((cols // 128, 8, 128), F32),
            pltpu.VMEM((cols // own * run, 128), F32),
            pltpu.SemaphoreType.DMA((steps, 4)),
            pltpu.SemaphoreType.DMA(()),
        ],
        compiler_params=pltpu.CompilerParams(vmem_limit_bytes=20 << 20),
        name="gate",
    )(in_hbm(projected), in_hbm(long_filter), in_hbm(short_filter))


def dot(a, b):
    return jnp.dot(a, b, preferred_element_type=F32)


def spectral_kernel(
    outer, z_ref, taps_ref, first_ref, fwd_ref, bwd_ref, last_ref, tc_ref, ts_ref, hc_ref, hs_ref,
    out_ref, rows_ref, fix_ref, spec_ref, half_ref, half_out_ref, prod_ref, back_ref, conv_ref, block_ref, sem,
):
    segments, own, tok = out_ref.shape
    both = 2 * own
    pitch = both + EXTRA
    out_pitch = conv_ref.shape[0] // segments
    piece = 16
    rim = outer * pitch

    def widen(i, carry):
        start = pl.multiple_of(i * (piece * pitch), piece * pitch)
        block = z_ref[pl.ds(start, piece * pitch), :].astype(F32)
        rows_ref[pl.ds(rim + start, piece * pitch), :] = block
        return carry

    lax.fori_loop(0, segments // piece, widen, 0)

    rows_ref[pitch - 1 : pitch, :] = jnp.zeros((1, tok), F32)
    for o in range(1, outer):
        last = (segments + o - 1) * pitch + pitch - 1
        rows_ref[o * pitch + pitch - 1 : (o + 1) * pitch, :] = rows_ref[last : last + 1, :]
    now = rows_ref[pl.ds(rim + both, segments, stride=pitch), :]
    ago = rows_ref[pl.ds(both + 1, segments, stride=pitch), :]
    lane = lax.broadcasted_iota(jnp.int32, (segments, tok), 1)
    middle = jnp.where(
        lane // own % 2 == 0, pltpu.roll(ago, tok - own, 1), pltpu.roll(now, own, 1)
    )
    edges = taps_ref[0:1, :] * now + taps_ref[1:2, :] * middle + taps_ref[2:3, :] * ago
    edges = edges * pltpu.roll(edges, tok - 2 * own, 1)
    after = pltpu.roll(edges, tok - own + 1, 1)
    fix_ref[0] = jnp.where(lane % 2 == 0, edges, after)
    fix_ref[1] = jnp.where(lane % 2 == 1, edges, after)

    top = 8
    index = lax.broadcasted_iota(jnp.int32, (top, tok), 0)

    def first_row(row, block):
        return jnp.concatenate([jnp.where(index == 0, row, block[:top]), block[top:]], 0)

    group, group2, group3, group4 = 32, 32, 16, 32

    run = 16

    def first_section(which, i, carry):
        start = i * group
        base = which * own + start
        cols = []
        for j in range(group):
            col = rows_ref[pl.ds(rim + base + j, segments, stride=pitch), :]
            if which == 0:
                fixed = pltpu.roll(fix_ref[j % 2], (tok - start - j) % tok, 1)
                col = jnp.where(lane < 2, fixed, col)
            cols.append(col.astype(BF16))
        out = dot(first_ref[...], jnp.concatenate(cols, 1))
        out = out.reshape(segments // top, 2, top, group * tok)
        tc, ts = tc_ref[...], ts_ref[...]
        for j in range(group):
            real = out[:, 0, :, j * tok : (j + 1) * tok].reshape(segments, tok)
            imag = out[:, 1, :, j * tok : (j + 1) * tok].reshape(segments, tok)
            half_ref[pl.ds(base + j, 1), :] = imag[0:1]
            imag = first_row(0.0, imag)
            both_parts = jnp.concatenate([real * tc + imag * ts, imag * tc - real * ts], 1)
            both_parts = both_parts.astype(BF16).reshape(segments // run, run, 2 * tok)
            spec_ref[start + j, :, which] = both_parts
        return carry

    for which in range(2):
        lax.fori_loop(0, own // group, functools.partial(first_section, which), 0)

    def product(sig, fil):
        sr, si, fr, fi = sig[:, :tok], sig[:, tok:], fil[:, :tok], fil[:, tok:]
        return jnp.concatenate(
            [(sr * fr - si * fi).astype(BF16), (sr * fi + si * fr).astype(BF16)], 1
        )

    half = half_ref[...]
    hc, hs = hc_ref[...], hs_ref[...]
    half = jnp.concatenate([(half * hc).astype(BF16), (-half * hs).astype(BF16)], 1)
    half = dot(half, fwd_ref[...])
    half = dot(product(half[:own], half[own:]), bwd_ref[...])
    half_out_ref[...] = half[:, :tok] * hc - half[:, tok:] * hs

    def multiply(i, carry):
        start = i * group2
        spec = spec_ref[pl.ds(start, group2)].reshape(group2 * 2 * segments, 2 * tok)
        spec = dot(spec, fwd_ref[...]).reshape(group2 * segments // run, 2, run, 2 * tok)
        sig = spec[:, 0].reshape(group2 * segments, 2 * tok)
        fil = spec[:, 1].reshape(group2 * segments, 2 * tok)
        prod_ref[pl.ds(start, group2)] = product(sig, fil).reshape(group2, segments, 2 * tok)
        return carry

    lax.fori_loop(0, own // group2, multiply, 0)

    def invert(i, carry):
        start = i * group3
        tc, ts = tc_ref[...], ts_ref[...]
        back = dot(
            prod_ref[pl.ds(start, group3)].reshape(group3 * segments, 2 * tok), bwd_ref[...]
        )
        for j in range(group3):
            br = back[j * segments : (j + 1) * segments, :tok]
            bi = back[j * segments : (j + 1) * segments, tok:]
            imag = first_row(half_out_ref[pl.ds(start + j, 1), :], bi * tc + br * ts)
            back_ref[start + j, :segments] = (br * tc - bi * ts).astype(BF16)
            back_ref[start + j, segments:] = imag.astype(BF16)
        return carry

    lax.fori_loop(0, own // group3, invert, 0)

    def finish(i, carry):
        start = i * group4
        stacked = jnp.concatenate([back_ref[start + j] for j in range(group4)], 1)
        conv = dot(last_ref[...], stacked)
        for j in range(group4):
            conv_ref[pl.ds(start + j, segments, stride=out_pitch), :] = conv[
                :, j * tok : (j + 1) * tok
            ]
        return carry

    lax.fori_loop(0, own // group4, finish, 0)

    def write(i):
        at = pl.ds(i * piece, piece)
        return pltpu.make_async_copy(block_ref.at[at], out_ref.at[at], sem.at[i])

    for i in range(segments // piece):
        for b in range(i * piece, (i + 1) * piece):
            block_ref[b] = conv_ref[b * out_pitch : b * out_pitch + own, :].astype(BF16)
        write(i).start()
    for i in range(segments // piece):
        write(i).wait()


def spectral(received, taps, consts, outer, own):
    tok = received.shape[1]
    both = 2 * own
    pitch = both + EXTRA
    segments = received.shape[0] // pitch
    return pl.pallas_call(
        functools.partial(spectral_kernel, outer),
        out_shape=pltpu.HBM((segments, own, tok), BF16),
        in_specs=[pl.BlockSpec(memory_space=pltpu.VMEM)] * 10,
        out_specs=pl.BlockSpec(memory_space=pltpu.HBM),
        scratch_shapes=[
            pltpu.VMEM(((segments + outer) * pitch, tok), F32),
            pltpu.VMEM((2, segments, tok), F32),
            pltpu.VMEM((own, segments // 16, 2, 16, 2 * tok), BF16),
            pltpu.VMEM((both, tok), F32),
            pltpu.VMEM((own, tok), F32),
            pltpu.VMEM((own, segments, 2 * tok), BF16),
            pltpu.VMEM((own, 2 * segments, tok), BF16),
            pltpu.VMEM((segments * (own + PAD), tok), F32),
            pltpu.VMEM((segments, own, tok), BF16),
            pltpu.SemaphoreType.DMA((segments // 16,)),
        ],
        compiler_params=pltpu.CompilerParams(vmem_limit_bytes=28 << 20),
        name="spectral",
    )(resident(received), taps, *consts)


def mix_kernel(c_ref, q_ref, skip_ref, g_ref, out_ref, buf_ref, sem):
    peers, own, tok = c_ref.shape
    steps = sem.shape[0]
    peers = peers // steps
    cols = peers * own
    near = 128 // own

    def write(i):
        at = pl.ds(i * cols, cols)
        return pltpu.make_async_copy(buf_ref.at[:, at], out_ref.at[:, at], sem.at[i])

    for i in range(steps):
        for j in range(i * peers, (i + 1) * peers, near):
            at = slice(j * own, (j + near) * own)
            conv = c_ref[j : j + near].reshape(near * own, tok).T.astype(F32)
            direct = skip_ref[:, at] * g_ref[:, at].astype(F32)
            buf_ref[:, at] = (q_ref[:, at].astype(F32) * (conv + direct)).astype(BF16)
        write(i).start()
    for i in range(steps):
        write(i).wait()


def resident(value):
    return pltpu.with_memory_space_constraint(value, pltpu.VMEM)


def mix(conv, query, skip, gated):
    devices, own, tok = conv.shape
    width = devices * own
    steps = 4
    return pl.pallas_call(
        mix_kernel,
        in_specs=[pl.BlockSpec(memory_space=pltpu.VMEM)] * 4,
        out_specs=pl.BlockSpec(memory_space=pltpu.HBM),
        out_shape=jax.ShapeDtypeStruct((tok, width), BF16),
        scratch_shapes=[
            pltpu.VMEM((tok, width), BF16),
            pltpu.SemaphoreType.DMA((steps,)),
        ],
        compiler_params=pltpu.CompilerParams(vmem_limit_bytes=6 << 20),
        name="mix",
    )(resident(conv), resident(query), resident(skip), resident(gated))


def side_kernel(q_ref, k_ref, v_ref, rq_ref, rk_ref, rv_ref, wq_ref, wk_ref, wv_ref,
                query_ref, gated_ref):
    def featurized(rows_ref, rim_ref, taps_ref):
        rows = rows_ref[...].astype(F32)
        rim = rim_ref[...].astype(F32)
        taps = taps_ref[...].astype(F32)
        index = lax.broadcasted_iota(jnp.int32, rows.shape, 0)
        back1 = jnp.where(index == 0, rim[1:2], pltpu.roll(rows, 1, 0))
        back2 = pltpu.roll(rows, 2, 0)
        back2 = jnp.where(index == 0, rim[0:1], jnp.where(index == 1, rim[1:2], back2))
        return taps[0:1] * rows + taps[1:2] * back1 + taps[2:3] * back2

    query_ref[...] = featurized(q_ref, rq_ref, wq_ref).astype(BF16)
    gated = featurized(k_ref, rk_ref, wk_ref) * featurized(v_ref, rv_ref, wv_ref)
    gated_ref[...] = gated.astype(BF16)


def side(projected, rim, short_filter):
    tok = projected.shape[0]
    width = projected.shape[1] // 3
    steps = 8
    cols = width // steps

    def thirds(rows):
        return [
            pl.BlockSpec((rows, cols), functools.partial(lambda third, i: (0, i + third * steps), t))
            for t in range(3)
        ]

    wide = pl.BlockSpec((tok, cols), lambda i: (0, i))
    return pl.pallas_call(
        side_kernel,
        grid=(steps,),
        in_specs=thirds(tok)
        + thirds(rim.shape[0])
        + thirds(short_filter.shape[0]),
        out_specs=[wide, wide],
        out_shape=[
            jax.ShapeDtypeStruct((tok, width), BF16),
            jax.ShapeDtypeStruct((tok, width), BF16),
        ],
        compiler_params=pltpu.CompilerParams(vmem_limit_bytes=8 << 20),
        name="side",
    )(*[in_hbm(projected)] * 3, *[rim] * 3, *[short_filter] * 3)


def shards(projected, short_filter, long_filter, skip):
    devices = lax.axis_size(AXES)
    tok, width = long_filter.shape
    own = width // devices
    tap_count = short_filter.shape[0]
    rim_count = tap_count - 1
    outer = lax.axis_size("outer")
    order = np.arange(devices).reshape(outer, -1).T.reshape(-1)
    consts = tables(order, tok)
    position = lax.axis_index(TURNED)
    taps = [
        lax.dynamic_slice_in_dim(short_filter, third * width + position * own, own, 1)
        for third in (1, 2)
    ]
    taps = jnp.concatenate([taps[0], taps[0], taps[1], taps[1]], 1).astype(F32)
    send = gate(projected, short_filter, long_filter, devices)
    pairs = send.reshape(devices, -1, 2, tok)
    received = lax.all_to_all(pairs, TURNED, split_axis=0, concat_axis=0, tiled=True)
    received = received.reshape(send.shape)
    rim = lax.ppermute(projected[tok - rim_count :], AXES, [(i, i + 1) for i in range(devices - 1)])
    query, gated = side(projected, rim, short_filter)
    conv = spectral(received, taps, consts, outer, own)
    conv = lax.all_to_all(conv, TURNED, split_axis=0, concat_axis=0, tiled=True)
    return mix(conv, query, skip[None, :], gated)


def solution(mesh):
    in_specs = (P(AXES, None), P(), P(AXES, None), P())
    return jax.shard_map(
        shards, mesh=mesh, in_specs=in_specs, out_specs=P(AXES, None), check_vma=False
    )
```
